32 devices in a mesh: dp: 4 (over y, x), ctx: 2 (over core), tp: 4 (over z).
Axes of the slice: x: 2, y: 2, z: 4, core: 2. Of those that a mesh axis runs over, the one named last changes fastest.
Arguments:
- query_branch: bfloat16 [2048, 8192], P(('dp', 'ctx'), 'tp'), parts along dimension 0, may hold values from -6 to 6
- key_branch: bfloat16 [2048, 8192], P(('dp', 'ctx'), 'tp'), parts along dimension 0, may hold values from -6 to 6
- value_branch: bfloat16 [2048, 8192], P(('dp', 'ctx'), 'tp'), parts along dimension 0, may hold values from -6 to 6
- output_grad: bfloat16 [2048, 8192], P(('dp', 'ctx'), 'tp'), parts along dimension 0, may hold values from -6 to 6
- residues: float32 [8192, 8], P('tp'), may hold values from -4 to 4
- decay_rates: float32 [8192, 8], P('tp'), as said below
Outputs:
- mixed_out: bfloat16 [2048, 8192], P(('dp', 'ctx'), 'tp'), parts along dimension 0
- query_grad: bfloat16 [2048, 8192], P(('dp', 'ctx'), 'tp'), parts along dimension 0
- key_grad: bfloat16 [2048, 8192], P(('dp', 'ctx'), 'tp'), parts along dimension 0
- value_grad: bfloat16 [2048, 8192], P(('dp', 'ctx'), 'tp'), parts along dimension 0
- residue_grad: float32 [32768, 8], P(('dp', 'tp')), parts along dimension 0
The draws below stay inside these ranges and needn't reach their ends.
There are 4 independent parts, one for each index of `dp`. The reference program is written for one: setup_inputs(seed, part) draws one part's arguments, and reference() takes and returns one part's arrays. A program takes and returns all parts, laid end to end along the dimension named above; an argument that names none is the same for every part. Nothing has to cross between parts.
Inputs may be any that keep to these rules, and one draw needn't show every extreme that they name: `decay_rates`: every rate lies between 0.5 / 512 and 100 / 512.
All inputs are finite; a program needn't handle non-finite values.
Results may differ from the reference program's by a relative error of at most 0.01.
Values may be sent and summed in bfloat16 or wider, within the bound.
No kernel may reach another device: no remote copies, remote signals or barrier semaphores. Data moves between devices by JAX's collectives and lax.ppermute only.
A program may use at most 128 MiB of HBM per device.

```python
import jax
import jax.numpy as jnp
from jax import lax

D = 8192
MODES = 8
TOKENS = 512


def clipped_normal(key):
    values = jax.random.normal(key, (TOKENS, D), jnp.float32)
    return jnp.clip(values, -6.0, 6.0)


def draw_key_branch(key, part):
    values = clipped_normal(jax.random.fold_in(key, 11))
    return values.astype(jnp.bfloat16)


def draw_output_grad(key, part):
    values = clipped_normal(jax.random.fold_in(key, 23))
    return values.astype(jnp.bfloat16)


def draw_decay_rates(key, part):
    fraction = jax.random.uniform(jax.random.fold_in(key, 37), (D, MODES), jnp.float32)
    lowest = jnp.log(0.5)
    highest = jnp.log(100.0)
    scaled = jnp.exp(lowest + fraction * (highest - lowest))
    return (scaled / TOKENS).astype(jnp.float32)


def level_of(stream_key, dims, pieces, low, high):
    level, own = 1.0, jax.random.fold_in(stream_key, 6)
    for axis_at, parts in pieces:
        heights = jnp.exp(jax.random.uniform(jax.random.fold_in(own, axis_at), (parts,), jnp.float32, low / len(pieces), high / len(pieces)))
        level = level * jnp.repeat(heights, dims[axis_at] // parts).reshape([-1 if axis == axis_at else 1 for axis in range(len(dims))])
    return level


def noise(key, dims, spread, limit, split=(), kind=jnp.bfloat16):
    array = spread * jax.random.normal(key, dims, jnp.float32)
    if split:
        array = array * level_of(key, dims, split, -0.22, 0.18)
    return jnp.clip(array, -limit, limit).astype(kind)


def setup_inputs(seed: int = 0, part: int = 0) -> dict:
    arg_keys = jax.random.split(jax.random.key(seed), 7)
    part_splits = jax.random.split(jax.random.fold_in(arg_keys[6], part), 7)
    return {
        "query_branch": noise(part_splits[0], (TOKENS, D), 1.0, 6.0, ((0, 2), (1, 4))),
        "key_branch": draw_key_branch(jax.random.fold_in(jax.random.fold_in(arg_keys[6], part), 71), part),
        "value_branch": noise(part_splits[2], (TOKENS, D), 1.0, 6.0, ((0, 2), (1, 4))),
        "output_grad": draw_output_grad(jax.random.fold_in(jax.random.fold_in(arg_keys[6], part), 71), part),
        "residues": noise(arg_keys[4], (D, MODES), 1.0, 4.0, ((0, 4),), jnp.float32),
        "decay_rates": draw_decay_rates(jax.random.fold_in(arg_keys[6], 71), part),
    }


def reference(query_branch, key_branch, value_branch, output_grad, residues, decay_rates):
    mixed_in = (key_branch.astype(jnp.float32) * value_branch.astype(jnp.float32)).astype(jnp.bfloat16)
    conv_grad = (output_grad.astype(jnp.float32) * query_branch.astype(jnp.float32)).astype(jnp.bfloat16)
    mixed_wide = mixed_in.astype(jnp.float32)
    grad_wide = conv_grad.astype(jnp.float32)
    sequence = mixed_in.shape[0]
    fft_size = 2 * sequence
    mode_scale = jnp.sqrt(-jnp.expm1(-2.0 * decay_rates) / MODES)
    weights = residues * mode_scale
    lag_index = jnp.arange(sequence, dtype=jnp.float32)[:, None]
    filter_sum = jnp.zeros(mixed_wide.shape, jnp.float32)
    for mode_index in range(MODES):
        filter_sum = filter_sum + weights[:, mode_index][None, :] * jnp.exp(-decay_rates[:, mode_index][None, :] * lag_index)
    in_spec = jnp.fft.rfft(mixed_wide, n=fft_size, axis=0)
    filter_spec = jnp.fft.rfft(filter_sum, n=fft_size, axis=0)
    conv = jnp.fft.irfft(filter_spec * in_spec, n=fft_size, axis=0)[:sequence]
    flipped_grad = grad_wide[::-1]
    flipped_spec = jnp.fft.rfft(flipped_grad, n=fft_size, axis=0)
    input_grad = jnp.fft.irfft(filter_spec * flipped_spec, n=fft_size, axis=0)[:sequence][::-1]
    residue_cols = []
    for mode_index in range(MODES):
        kernel = jnp.exp(-decay_rates[:, mode_index][None, :] * lag_index)
        response = jnp.fft.irfft(jnp.fft.rfft(kernel, n=fft_size, axis=0) * in_spec, n=fft_size, axis=0)[:sequence]
        residue_cols.append(mode_scale[:, mode_index] * lax.optimization_barrier(jnp.sum(grad_wide * response, axis=0)))
    residue_grad = jnp.stack(residue_cols, axis=1)
    mixed_out = (query_branch.astype(jnp.float32) * conv).astype(jnp.bfloat16)
    query_grad = (output_grad.astype(jnp.float32) * conv).astype(jnp.bfloat16)
    key_grad = (input_grad * value_branch.astype(jnp.float32)).astype(jnp.bfloat16)
    value_grad = (input_grad * key_branch.astype(jnp.float32)).astype(jnp.bfloat16)
    return (mixed_out, query_grad, key_grad, value_grad, residue_grad)
```

```python
import functools

import jax
import jax.numpy as jnp
from jax import lax
from jax.experimental import pallas as pl
from jax.experimental.pallas import tpu as pltpu
from jax.sharding import PartitionSpec as P

F32 = jnp.float32
BF16 = jnp.bfloat16
LANES = 128
GROUPS = 8
BLOCK = GROUPS * LANES
PAD = 8
UNROLL = 8


def one_minus_exp_2(rate, factor):
    square = rate * rate
    sinh = rate * (1.0 + square * (1 / 6 + square * (1 / 120 + square * (1 / 5040))))
    return 2.0 * factor * sinh


def mode_tables(rates, residues, table):
    modes, channels = rates.shape
    factor = jnp.exp(-rates)
    scale = jnp.sqrt(one_minus_exp_2(rates, factor) / modes)
    weight = residues * scale
    groups = channels // LANES
    for group in range(groups):
        lanes = slice(group * LANES, (group + 1) * LANES)
        table[pl.ds(group * modes, modes), :] = factor[:, lanes]
        table[pl.ds((groups + group) * modes, modes), :] = weight[:, lanes]
    return scale


def table_rows(table, which, half, modes, groups):
    start = (which * groups + half * GROUPS) * modes
    return [table[pl.ds(start + mode, GROUPS, stride=modes), :] for mode in range(modes)]


def tree_sum(terms):
    while len(terms) > 1:
        terms = [
            terms[i] + terms[i + 1] if i + 1 < len(terms) else terms[i]
            for i in range(0, len(terms), 2)
        ]
    return terms[0]


class Shape:
    def __init__(self, length, channels, modes):
        self.length = length
        self.channels = channels
        self.modes = modes
        self.halves = channels // BLOCK
        self.groups = channels // LANES
        self.chunk = min(64, length)
        self.chunks = length // self.chunk
        self.stride = length + PAD
        self.rows = self.halves * GROUPS * self.stride


def lanes_of(half):
    return slice(half * BLOCK, (half + 1) * BLOCK)


def products(shape, half, token, inputs, wide):
    step = min(32, shape.chunk)

    def body(i, carry):
        at = pl.multiple_of(token + i * step, step)
        for group in range(GROUPS):
            lane = slice(half * BLOCK + group * LANES, half * BLOCK + (group + 1) * LANES)
            row = pl.multiple_of((half * GROUPS + group) * shape.stride + at, 8)
            q, dy, v, k = [inputs[j, pl.ds(at, step), lane] for j in range(4)]
            wide[0, pl.ds(row, step), :] = (k * v).astype(F32)
            wide[1, pl.ds(row, step), :] = (dy * q).astype(F32)
        return carry

    lax.fori_loop(0, shape.chunk // step, body, 0)


def recurrence(shape, half, direction, chunk_index, factor, weight, state, dot, wide, conv):
    sign = 1 - 2 * direction
    begin = direction * (shape.length - 1) + sign * chunk_index * shape.chunk
    base = half * GROUPS * shape.stride
    modes = shape.modes

    def body(i, carry):
        state, dot = list(carry[0]), list(carry[1])
        for j in range(UNROLL):
            row = base + begin + sign * (i * UNROLL + j)
            rows = pl.ds(row, GROUPS, stride=shape.stride)
            source = wide[direction, rows, :]
            other = wide[1 - direction, rows, :] if dot else None
            terms = []
            for mode in range(modes):
                state[mode] = factor[mode] * state[mode] + source
                if weight is not None:
                    terms.append(weight[mode] * state[mode])
                if dot:
                    dot[mode] = dot[mode] + other * state[mode]
            if weight is not None:
                conv[rows, :] = tree_sum(terms)
        return tuple(state), tuple(dot)

    state, dot = lax.fori_loop(0, shape.chunk // UNROLL, body, (tuple(state), tuple(dot)))
    return list(state), list(dot)


def outputs(shape, half, token, pair, inputs, conv, staged):
    step = min(32, shape.chunk)

    def body(i, carry):
        at = pl.multiple_of(token + i * step, step)
        for group in range(GROUPS):
            lane = slice(half * BLOCK + group * LANES, half * BLOCK + (group + 1) * LANES)
            row = pl.multiple_of((half * GROUPS + group) * shape.stride + at, 8)
            value = conv[pl.ds(row, step), :]
            for j in range(2):
                staged[j, pl.ds(at, step), lane] = (
                    inputs[2 * pair + j, pl.ds(at, step), lane].astype(F32) * value
                ).astype(BF16)
        return carry

    lax.fori_loop(0, shape.chunk // step, body, 0)


def token_of(shape, direction, chunk_index):
    last = shape.chunks - 1
    return pl.multiple_of(
        (chunk_index + direction * (last - 2 * chunk_index)) * shape.chunk, shape.chunk
    )


def in_copy(shape, j, half, direction, chunk, source, inputs, sem):
    where = (pl.ds(token_of(shape, direction, chunk), shape.chunk), lanes_of(half))
    return pltpu.make_async_copy(
        source.at[where], inputs.at[(j,) + where], sem.at[j, half * shape.chunks + chunk]
    )


def out_copy(shape, j, half, direction, chunk, staged, target, sem):
    where = (pl.ds(token_of(shape, direction, chunk), shape.chunk), lanes_of(half))
    return pltpu.make_async_copy(
        staged.at[(j,) + where], target.at[where], sem.at[j, half * shape.chunks + chunk]
    )


def send_out(shape, half, pair, direction, chunk, staged, targets, sem):
    for p in range(2):

        @pl.when(pair == p)
        def _():
            for j in range(2):
                out_copy(shape, j, half, direction, chunk, staged, targets[2 * p + j], sem).start()


def wait_out(shape, direction, staged, targets, sem):
    for half in range(shape.halves):
        for chunk in range(shape.chunks):
            for j in range(2):
                out_copy(shape, j, half, direction, chunk, staged, targets[j], sem).wait()


def first_kernel(
    shape, q, dy, v, k, rates_hbm, res_hbm,
    out0, out1, out2, out3, wide, inputs, sent, table, scale,
    conv, staged, rates, res, in_sem, coef_sem, out_sem,
):
    direction = lax.axis_index("ctx")
    sources = (q, dy, v, k)
    targets = (out0, out1, out2, out3)
    coef = [
        pltpu.make_async_copy(rates_hbm, rates, coef_sem.at[0]),
        pltpu.make_async_copy(res_hbm, res, coef_sem.at[1]),
    ]
    for copy in coef:
        copy.start()
    for half in range(shape.halves):
        for chunk in range(shape.chunks):
            for j in range(4):
                in_copy(shape, j, half, direction, chunk, sources[j], inputs, in_sem).start()
    for copy in coef:
        copy.wait()
    scale[...] = mode_tables(rates[...], res[...], table)
    zero = jnp.zeros((GROUPS, LANES), F32)
    for half in range(shape.halves):
        factor = table_rows(table, 0, half, shape.modes, shape.groups)
        weight = table_rows(table, 1, half, shape.modes, shape.groups)

        def body(chunk, carry):
            token = token_of(shape, direction, chunk)
            for j in range(4):
                in_copy(shape, j, half, direction, chunk, sources[j], inputs, in_sem).wait()
            products(shape, half, token, inputs, wide)
            state, dot = recurrence(
                shape, half, direction, chunk, factor, weight, carry[0], carry[1], wide, conv
            )
            outputs(shape, half, token, direction, inputs, conv, staged)
            send_out(shape, half, direction, direction, chunk, staged, targets, out_sem)
            return tuple(state), tuple(dot)

        zeros = (zero,) * shape.modes
        state, dot = lax.fori_loop(0, shape.chunks, body, (zeros, zeros))
        rows = slice(half * GROUPS, (half + 1) * GROUPS)
        for mode in range(shape.modes):
            sent[0, mode, rows, :] = state[mode].astype(BF16)
            sent[1, mode, rows, :] = dot[mode].astype(BF16)
    wait_out(shape, direction, staged, targets, out_sem)


def second_kernel(
    shape, in0, in1, in2, in3, wide, inputs, sent, table, scale, received,
    out0, out1, out2, out3, residue,
    conv, staged, totals, out_sem,
):
    del in0, in1, in2, in3
    direction = 1 - lax.axis_index("ctx")
    targets = (out0, out1, out2, out3)
    modes = shape.modes
    for half in range(shape.halves):
        rows = slice(half * GROUPS, (half + 1) * GROUPS)
        factor = table_rows(table, 0, half, modes, shape.groups)
        weight = table_rows(table, 1, half, modes, shape.groups)
        state = []
        for mode in range(modes):
            mine = sent[0, mode, rows, :].astype(F32)
            theirs = received[0, mode, rows, :].astype(F32)
            dots = sent[1, mode, rows, :].astype(F32) + received[1, mode, rows, :].astype(F32)
            totals[pl.ds((half * modes + mode) * GROUPS, GROUPS), :] = (
                dots + factor[mode] * (mine * theirs)
            )
            state.append(theirs)
        for group in range(GROUPS):
            lane = slice(half * BLOCK + group * LANES, half * BLOCK + (group + 1) * LANES)
            picked = totals[pl.ds(half * modes * GROUPS + group, modes, stride=GROUPS), :]
            residue[:, lane] = picked * scale[:, lane]

        def body(chunk, state):
            token = token_of(shape, direction, chunk)
            state, _ = recurrence(
                shape, half, direction, chunk, factor, weight, state, (), wide, conv
            )
            outputs(shape, half, token, direction, inputs, conv, staged)
            send_out(shape, half, direction, direction, chunk, staged, targets, out_sem)
            return tuple(state)

        lax.fori_loop(0, shape.chunks, body, tuple(state))
    wait_out(shape, direction, staged, targets, out_sem)


def ends_kernel(
    shape, q, dy, v, k, rates_hbm, res_hbm,
    wide, inputs, ends, table, scale,
    rates, res, in_sem, coef_sem,
):
    sources = (q, dy, v, k)
    coef = [
        pltpu.make_async_copy(rates_hbm, rates, coef_sem.at[0]),
        pltpu.make_async_copy(res_hbm, res, coef_sem.at[1]),
    ]
    for copy in coef:
        copy.start()
    for half in range(shape.halves):
        for chunk in range(shape.chunks):
            for j in range(4):
                in_copy(shape, j, half, 0, chunk, sources[j], inputs, in_sem).start()
    for copy in coef:
        copy.wait()
    scale[...] = mode_tables(rates[...], res[...], table)
    zeros = (jnp.zeros((GROUPS, LANES), F32),) * shape.modes
    for half in range(shape.halves):
        factor = table_rows(table, 0, half, shape.modes, shape.groups)

        def forward(chunk, carry):
            for j in range(4):
                in_copy(shape, j, half, 0, chunk, sources[j], inputs, in_sem).wait()
            products(shape, half, token_of(shape, 0, chunk), inputs, wide)
            state, dot = recurrence(
                shape, half, 0, chunk, factor, None, carry[0], carry[1], wide, None
            )
            return tuple(state), tuple(dot)

        def backward(chunk, state):
            state, _ = recurrence(shape, half, 1, chunk, factor, None, state, (), wide, None)
            return tuple(state)

        state, dot = lax.fori_loop(0, shape.chunks, forward, (zeros, zeros))
        back = lax.fori_loop(0, shape.chunks, backward, zeros)
        rows = slice(half * GROUPS, (half + 1) * GROUPS)
        for mode in range(shape.modes):
            ends[0, mode, rows, :] = state[mode]
            ends[1, mode, rows, :] = back[mode]
            ends[2, mode, rows, :] = dot[mode]


def both_kernel(
    shape, wide, inputs, starts, table,
    out0, out1, out2, out3,
    conv, staged, out_sem,
):
    targets = (out0, out1, out2, out3)
    for direction in range(2):
        for half in range(shape.halves):
            rows = slice(half * GROUPS, (half + 1) * GROUPS)
            factor = table_rows(table, 0, half, shape.modes, shape.groups)
            weight = table_rows(table, 1, half, shape.modes, shape.groups)
            state = tuple(starts[direction, mode, rows, :] for mode in range(shape.modes))

            def body(chunk, state):
                token = token_of(shape, direction, chunk)
                state, _ = recurrence(
                    shape, half, direction, chunk, factor, weight, state, (), wide, conv
                )
                outputs(shape, half, token, direction, inputs, conv, staged)
                for j in range(2):
                    out_copy(
                        shape, j, half, direction, chunk, staged, targets[2 * direction + j], out_sem
                    ).start()
                return tuple(state)

            lax.fori_loop(0, shape.chunks, body, state)
        wait_out(shape, direction, staged, targets[2 * direction :], out_sem)


HBM = pl.BlockSpec(memory_space=pltpu.HBM)
VMEM = pl.BlockSpec(memory_space=pltpu.VMEM)
LIMIT = 24 << 20


def pair(shape, arrays):
    modes, channels = shape.modes, shape.channels
    big = jax.ShapeDtypeStruct((shape.length, channels), BF16)
    copies = shape.halves * shape.chunks
    *outs, wide, inputs, sent, table, scale = pl.pallas_call(
        functools.partial(first_kernel, shape),
        in_specs=[HBM] * 6,
        out_specs=[HBM] * 4 + [VMEM] * 5,
        out_shape=[big] * 4
        + [
            pltpu.VMEM((2, shape.rows, LANES), F32),
            pltpu.VMEM((4, shape.length, channels), BF16),
            jax.ShapeDtypeStruct((2, modes, shape.groups, LANES), BF16),
            pltpu.VMEM((2 * modes * shape.groups, LANES), F32),
            pltpu.VMEM((modes, channels), F32),
        ],
        scratch_shapes=[
            pltpu.VMEM((shape.rows, LANES), F32),
            pltpu.VMEM((2, shape.length, channels), BF16),
            pltpu.VMEM((modes, channels), F32),
            pltpu.VMEM((modes, channels), F32),
            pltpu.SemaphoreType.DMA((4, copies)),
            pltpu.SemaphoreType.DMA((2,)),
            pltpu.SemaphoreType.DMA((2, copies)),
        ],
        compiler_params=pltpu.CompilerParams(vmem_limit_bytes=LIMIT),
        name="first",
    )(*arrays)
    received = lax.ppermute(sent, "ctx", [(0, 1), (1, 0)])
    *outs, residue = pl.pallas_call(
        functools.partial(second_kernel, shape),
        in_specs=[HBM] * 4 + [VMEM] * 6,
        out_specs=[HBM] * 4 + [VMEM],
        out_shape=[big] * 4 + [jax.ShapeDtypeStruct((modes, channels), F32)],
        input_output_aliases={0: 0, 1: 1, 2: 2, 3: 3},
        scratch_shapes=[
            pltpu.VMEM((shape.rows, LANES), F32),
            pltpu.VMEM((2, shape.length, channels), BF16),
            pltpu.VMEM((modes * shape.groups, LANES), F32),
            pltpu.SemaphoreType.DMA((2, copies)),
        ],
        compiler_params=pltpu.CompilerParams(vmem_limit_bytes=LIMIT),
        name="second",
    )(*outs, wide, inputs, sent, table, scale, received)
    return outs, residue


def many(shape, arrays, rates, owners):
    modes, channels = shape.modes, shape.channels
    big = jax.ShapeDtypeStruct((shape.length, channels), BF16)
    copies = shape.halves * shape.chunks
    wide, inputs, ends, table, scale = pl.pallas_call(
        functools.partial(ends_kernel, shape),
        in_specs=[HBM] * 6,
        out_specs=[VMEM] * 5,
        out_shape=[
            pltpu.VMEM((2, shape.rows, LANES), F32),
            pltpu.VMEM((4, shape.length, channels), BF16),
            jax.ShapeDtypeStruct((3, modes, shape.groups, LANES), F32),
            pltpu.VMEM((2 * modes * shape.groups, LANES), F32),
            jax.ShapeDtypeStruct((modes, channels), F32),
        ],
        scratch_shapes=[
            pltpu.VMEM((modes, channels), F32),
            pltpu.VMEM((modes, channels), F32),
            pltpu.SemaphoreType.DMA((4, copies)),
            pltpu.SemaphoreType.DMA((2,)),
        ],
        compiler_params=pltpu.CompilerParams(vmem_limit_bytes=LIMIT),
        name="ends",
    )(*arrays)
    rates = rates.reshape(modes, shape.groups, LANES)
    here = lax.axis_index("ctx")
    parts = lax.all_gather(ends[:2].astype(BF16), "ctx", axis=0).astype(F32)
    owner = jnp.arange(owners, dtype=jnp.int32)
    gaps = jnp.stack([here - 1 - owner, owner - 1 - here], axis=1).astype(F32)[:, :, None, None, None]
    decay = jnp.exp(-rates * shape.length * jnp.maximum(gaps, 0.0))
    starts = jnp.sum(jnp.where(gaps >= 0, decay, 0.0) * parts, axis=0)
    dots = ends[2] + jnp.exp(-rates) * ends[1] * starts[0]
    total = jnp.sum(lax.all_gather(dots.astype(BF16), "ctx", axis=0).astype(F32), axis=0)
    residue = total.reshape(modes, channels) * scale
    outs = pl.pallas_call(
        functools.partial(both_kernel, shape),
        in_specs=[VMEM] * 4,
        out_specs=[HBM] * 4,
        out_shape=[big] * 4,
        scratch_shapes=[
            pltpu.VMEM((shape.rows, LANES), F32),
            pltpu.VMEM((2, shape.length, channels), BF16),
            pltpu.SemaphoreType.DMA((2, copies)),
        ],
        compiler_params=pltpu.CompilerParams(vmem_limit_bytes=LIMIT),
        name="both",
    )(wide, inputs, starts, table)
    return outs, residue


def body(owners, query_branch, key_branch, value_branch, output_grad, residues, decay_rates):
    length, channels = query_branch.shape
    rates = decay_rates.T
    shape = Shape(length, channels, rates.shape[0])
    hbm = functools.partial(pltpu.with_memory_space_constraint, memory_space=pltpu.HBM)
    arrays = [
        hbm(array)
        for array in (query_branch, output_grad, value_branch, key_branch, rates, residues.T)
    ]
    outs, residue = pair(shape, arrays) if owners == 2 else many(shape, arrays, rates, owners)
    mixed_out, query_grad, key_grad, value_grad = outs
    return (mixed_out, query_grad, key_grad, value_grad, residue.T)


def solution(mesh):
    tokens = P(("dp", "ctx"), "tp")
    return jax.shard_map(
        functools.partial(body, mesh.shape["ctx"]),
        mesh=mesh,
        in_specs=(tokens,) * 4 + (P("tp", None),) * 2,
        out_specs=(tokens,) * 4 + (P(("dp", "tp"), None),),
        check_vma=False,
    )
```

```python
import functools

import jax
import jax.numpy as jnp
from jax import lax
from jax.experimental import pallas as pl
from jax.experimental.pallas import tpu as pltpu
from jax.sharding import PartitionSpec as P

F32 = jnp.float32
BF16 = jnp.bfloat16
LANES = 128
GROUPS = 8
BLOCK = GROUPS * LANES
PAD = 8
UNROLL = 16


def one_minus_exp_2(rate, factor):
    square = rate * rate
    sinh = rate * (1.0 + square * (1 / 6 + square * (1 / 120 + square * (1 / 5040))))
    return 2.0 * factor * sinh


def mode_tables(rates, residues, table):
    modes, channels = rates.shape
    factor = jnp.exp(-rates)
    scale = jnp.sqrt(one_minus_exp_2(rates, factor) / modes)
    weight = residues * scale
    groups = channels // LANES
    for group in range(groups):
        lanes = slice(group * LANES, (group + 1) * LANES)
        table[pl.ds(group * modes, modes), :] = factor[:, lanes]
        table[pl.ds((groups + group) * modes, modes), :] = weight[:, lanes]
    return scale


def table_rows(table, which, half, modes, groups):
    start = (which * groups + half * GROUPS) * modes
    return [table[pl.ds(start + mode, GROUPS, stride=modes), :] for mode in range(modes)]


def tree_sum(terms):
    while len(terms) > 1:
        terms = [
            terms[i] + terms[i + 1] if i + 1 < len(terms) else terms[i]
            for i in range(0, len(terms), 2)
        ]
    return terms[0]


class Shape:
    def __init__(self, length, channels, modes):
        self.length = length
        self.channels = channels
        self.modes = modes
        self.halves = channels // BLOCK
        self.groups = channels // LANES
        self.chunk = min(64, length)
        self.chunks = length // self.chunk
        self.stride = length + PAD
        self.plane = GROUPS * self.stride
        self.rows = self.halves * self.plane


def lanes_of(half, group=None):
    if group is None:
        return pl.ds(pl.multiple_of(half * BLOCK, BLOCK), BLOCK)
    return pl.ds(pl.multiple_of(half * BLOCK + group * LANES, LANES), LANES)


def groups_of(half):
    return pl.ds(pl.multiple_of(half * GROUPS, GROUPS), GROUPS)


def products(shape, half, token, inputs, wide):
    step = min(32, shape.chunk)

    def body(i, carry):
        at = pl.multiple_of(token + i * step, step)
        for group in range(GROUPS):
            lane = slice(group * LANES, (group + 1) * LANES)
            row = half * shape.plane + group * shape.stride + at
            rows = pl.ds(pl.multiple_of(row, GROUPS), step)
            q, dy, v, k = [inputs[j, half, pl.ds(at, step), lane] for j in range(4)]
            wide[0, rows, :] = (k * v).astype(F32)
            wide[1, rows, :] = (dy * q).astype(F32)
        return carry

    lax.fori_loop(0, shape.chunk // step, body, 0)


def recurrence(shape, half, direction, chunk_index, factor, weight, state, dot, wide, conv):
    sign = 1 - 2 * direction
    begin = direction * (shape.length - 1) + sign * chunk_index * shape.chunk
    begin = half * shape.plane + begin
    steps = [sign * j for j in range(UNROLL)]
    stride = sign * UNROLL
    modes = shape.modes

    def body(i, carry):
        state, dot = list(carry[0]), list(carry[1])
        for j in range(UNROLL):
            rows = pl.ds(begin + i * stride + steps[j], GROUPS, stride=shape.stride)
            source = wide[direction, rows, :]
            other = wide[1 - direction, rows, :] if dot else None
            terms = []
            for mode in range(modes):
                state[mode] = factor[mode] * state[mode] + source
                if weight is not None:
                    terms.append(weight[mode] * state[mode])
                if dot:
                    dot[mode] = dot[mode] + other * state[mode]
            if weight is not None:
                conv[rows, :] = tree_sum(terms)
        return tuple(state), tuple(dot)

    state, dot = lax.fori_loop(0, shape.chunk // UNROLL, body, (tuple(state), tuple(dot)))
    return list(state), list(dot)


def outputs(shape, half, token, pair, inputs, conv, staged):
    step = min(32, shape.chunk)

    def body(i, carry):
        at = pl.multiple_of(token + i * step, step)
        for group in range(GROUPS):
            lane = slice(group * LANES, (group + 1) * LANES)
            row = half * shape.plane + group * shape.stride + at
            rows = pl.ds(pl.multiple_of(row, GROUPS), step)
            value = conv[rows, :]
            for j in range(2):
                staged[j, half, pl.ds(at, step), lane] = (
                    inputs[2 * pair + j, half, pl.ds(at, step), lane].astype(F32) * value
                ).astype(BF16)
        return carry

    lax.fori_loop(0, shape.chunk // step, body, 0)


def token_of(shape, direction, chunk_index):
    last = shape.chunks - 1
    return pl.multiple_of(
        (chunk_index + direction * (last - 2 * chunk_index)) * shape.chunk, shape.chunk
    )


def in_copy(shape, j, half, direction, chunk, source, inputs, sem):
    rows = pl.ds(token_of(shape, direction, chunk), shape.chunk)
    return pltpu.make_async_copy(
        source.at[rows, lanes_of(half)], inputs.at[j, half, rows, :], sem.at[j, half * shape.chunks + chunk]
    )


def out_copy(shape, j, half, direction, chunk, staged, target, sem):
    rows = pl.ds(token_of(shape, direction, chunk), shape.chunk)
    return pltpu.make_async_copy(
        staged.at[j, half, rows, :], target.at[rows, lanes_of(half)], sem.at[j, half * shape.chunks + chunk]
    )


def send_out(shape, half, pair, direction, chunk, staged, targets, sem):
    for p in range(2):

        @pl.when(pair == p)
        def _():
            for j in range(2):
                out_copy(shape, j, half, direction, chunk, staged, targets[2 * p + j], sem).start()


def wait_out(shape, direction, staged, targets, sem):
    for half in range(shape.halves):
        for chunk in range(shape.chunks):
            for j in range(2):
                out_copy(shape, j, half, direction, chunk, staged, targets[j], sem).wait()


def first_kernel(
    shape, q, dy, v, k, rates_hbm, res_hbm,
    conv, wide, inputs, sent, table, scale,
    rates, res, in_sem, coef_sem,
):
    direction = lax.axis_index("ctx")
    sources = (q, dy, v, k)
    coef = [
        pltpu.make_async_copy(rates_hbm, rates, coef_sem.at[0]),
        pltpu.make_async_copy(res_hbm, res, coef_sem.at[1]),
    ]
    for copy in coef:
        copy.start()
    for half in range(shape.halves):
        for chunk in range(shape.chunks):
            for j in range(4):
                in_copy(shape, j, half, direction, chunk, sources[j], inputs, in_sem).start()
    for copy in coef:
        copy.wait()
    scale[...] = mode_tables(rates[...], res[...], table)
    zeros = (jnp.zeros((GROUPS, LANES), F32),) * shape.modes

    def sweep(half, _):
        factor = table_rows(table, 0, half, shape.modes, shape.groups)
        weight = table_rows(table, 1, half, shape.modes, shape.groups)

        def body(chunk, carry):
            token = token_of(shape, direction, chunk)
            for j in range(4):
                in_copy(shape, j, half, direction, chunk, sources[j], inputs, in_sem).wait()
            products(shape, half, token, inputs, wide)
            state, dot = recurrence(
                shape, half, direction, chunk, factor, weight, carry[0], carry[1], wide, conv
            )
            return tuple(state), tuple(dot)

        state, dot = lax.fori_loop(0, shape.chunks, body, (zeros, zeros))
        for mode in range(shape.modes):
            sent[0, mode, groups_of(half), :] = state[mode].astype(BF16)
            sent[1, mode, groups_of(half), :] = dot[mode].astype(BF16)
        return 0

    lax.fori_loop(0, shape.halves, sweep, 0)


def early_kernel(shape, conv, inputs, staged):
    direction = lax.axis_index("ctx")

    def body(i, carry):
        half, chunk = i // shape.chunks, i % shape.chunks
        outputs(shape, half, token_of(shape, 0, chunk), direction, inputs, conv, staged)
        return carry

    lax.fori_loop(0, shape.halves * shape.chunks, body, 0)


def early_copy(j, half, early, target, sem):
    return pltpu.make_async_copy(
        early.at[j, half], target.at[:, lanes_of(half)], sem.at[j, half]
    )


def second_kernel(
    shape, early, wide, inputs, sent, table, scale, received,
    out0, out1, out2, out3, residue,
    conv, staged, totals, total, out_sem, early_sem, residue_sem,
):
    owner = lax.axis_index("ctx")
    direction = 1 - owner
    targets = (out0, out1, out2, out3)
    modes = shape.modes
    for p in range(2):

        @pl.when(owner == p)
        def _():
            for j in range(2):
                for half in range(shape.halves):
                    early_copy(j, half, early, targets[2 * p + j], early_sem).start()

    def sweep(half, _):
        factor = table_rows(table, 0, half, modes, shape.groups)
        weight = table_rows(table, 1, half, modes, shape.groups)
        state = []
        for mode in range(modes):
            mine = sent[0, mode, groups_of(half), :].astype(F32)
            theirs = received[0, mode, groups_of(half), :].astype(F32)
            mine_dot = sent[1, mode, groups_of(half), :].astype(F32)
            their_dot = received[1, mode, groups_of(half), :].astype(F32)
            totals[pl.ds(mode * GROUPS, GROUPS), :] = (
                mine_dot + their_dot + factor[mode] * (mine * theirs)
            )
            state.append(theirs)
        for group in range(GROUPS):
            lane = lanes_of(half, group)
            total[:, lane] = totals[pl.ds(group, modes, stride=GROUPS), :] * scale[:, lane]
        lane = lanes_of(half)
        pltpu.make_async_copy(total.at[:, lane], residue.at[:, lane], residue_sem.at[half]).start()

        def body(chunk, state):
            token = token_of(shape, direction, chunk)
            state, _ = recurrence(
                shape, half, direction, chunk, factor, weight, state, (), wide, conv
            )
            outputs(shape, half, token, direction, inputs, conv, staged)
            send_out(shape, half, direction, direction, chunk, staged, targets, out_sem)
            return tuple(state)

        lax.fori_loop(0, shape.chunks, body, tuple(state))
        return 0

    lax.fori_loop(0, shape.halves, sweep, 0)
    for j in range(2):
        for half in range(shape.halves):
            early_copy(j, half, early, targets[j], early_sem).wait()
    for half in range(shape.halves):
        lane = lanes_of(half)
        pltpu.make_async_copy(total.at[:, lane], residue.at[:, lane], residue_sem.at[half]).wait()
    wait_out(shape, direction, staged, targets, out_sem)


def ends_kernel(
    shape, q, dy, v, k, rates_hbm, res_hbm,
    wide, inputs, ends, table, scale,
    rates, res, in_sem, coef_sem,
):
    sources = (q, dy, v, k)
    coef = [
        pltpu.make_async_copy(rates_hbm, rates, coef_sem.at[0]),
        pltpu.make_async_copy(res_hbm, res, coef_sem.at[1]),
    ]
    for copy in coef:
        copy.start()
    for half in range(shape.halves):
        for chunk in range(shape.chunks):
            for j in range(4):
                in_copy(shape, j, half, 0, chunk, sources[j], inputs, in_sem).start()
    for copy in coef:
        copy.wait()
    scale[...] = mode_tables(rates[...], res[...], table)
    zeros = (jnp.zeros((GROUPS, LANES), F32),) * shape.modes
    for half in range(shape.halves):
        factor = table_rows(table, 0, half, shape.modes, shape.groups)

        def forward(chunk, carry):
            for j in range(4):
                in_copy(shape, j, half, 0, chunk, sources[j], inputs, in_sem).wait()
            products(shape, half, token_of(shape, 0, chunk), inputs, wide)
            state, dot = recurrence(
                shape, half, 0, chunk, factor, None, carry[0], carry[1], wide, None
            )
            return tuple(state), tuple(dot)

        def backward(chunk, state):
            state, _ = recurrence(shape, half, 1, chunk, factor, None, state, (), wide, None)
            return tuple(state)

        state, dot = lax.fori_loop(0, shape.chunks, forward, (zeros, zeros))
        back = lax.fori_loop(0, shape.chunks, backward, zeros)
        rows = groups_of(half)
        for mode in range(shape.modes):
            ends[0, mode, rows, :] = state[mode]
            ends[1, mode, rows, :] = back[mode]
            ends[2, mode, rows, :] = dot[mode]


def both_kernel(
    shape, wide, inputs, starts, table,
    out0, out1, out2, out3,
    conv, staged, out_sem,
):
    targets = (out0, out1, out2, out3)
    for direction in range(2):
        for half in range(shape.halves):
            rows = groups_of(half)
            factor = table_rows(table, 0, half, shape.modes, shape.groups)
            weight = table_rows(table, 1, half, shape.modes, shape.groups)
            state = tuple(starts[direction, mode, rows, :] for mode in range(shape.modes))

            def body(chunk, state):
                token = token_of(shape, direction, chunk)
                state, _ = recurrence(
                    shape, half, direction, chunk, factor, weight, state, (), wide, conv
                )
                outputs(shape, half, token, direction, inputs, conv, staged)
                for j in range(2):
                    out_copy(
                        shape, j, half, direction, chunk, staged, targets[2 * direction + j], out_sem
                    ).start()
                return tuple(state)

            lax.fori_loop(0, shape.chunks, body, state)
        wait_out(shape, direction, staged, targets[2 * direction :], out_sem)


HBM = pl.BlockSpec(memory_space=pltpu.HBM)
VMEM = pl.BlockSpec(memory_space=pltpu.VMEM)
LIMIT = 24 << 20


def pair(shape, arrays):
    modes, channels = shape.modes, shape.channels
    big = jax.ShapeDtypeStruct((shape.length, channels), BF16)
    copies = shape.halves * shape.chunks
    conv, wide, inputs, sent, table, scale = pl.pallas_call(
        functools.partial(first_kernel, shape),
        in_specs=[HBM] * 6,
        out_specs=[VMEM] * 6,
        out_shape=[
            pltpu.VMEM((shape.rows, LANES), F32),
            pltpu.VMEM((2, shape.rows, LANES), F32),
            pltpu.VMEM((4, shape.halves, shape.length, BLOCK), BF16),
            jax.ShapeDtypeStruct((2, modes, shape.groups, LANES), BF16),
            pltpu.VMEM((2 * modes * shape.groups, LANES), F32),
            pltpu.VMEM((modes, channels), F32),
        ],
        scratch_shapes=[
            pltpu.VMEM((modes, channels), F32),
            pltpu.VMEM((modes, channels), F32),
            pltpu.SemaphoreType.DMA((4, copies)),
            pltpu.SemaphoreType.DMA((2,)),
        ],
        compiler_params=pltpu.CompilerParams(vmem_limit_bytes=LIMIT),
        name="first",
    )(*arrays)
    received = lax.ppermute(sent, "ctx", [(0, 1), (1, 0)])
    early = pl.pallas_call(
        functools.partial(early_kernel, shape),
        in_specs=[VMEM] * 2,
        out_specs=VMEM,
        out_shape=pltpu.VMEM((2, shape.halves, shape.length, BLOCK), BF16),
        compiler_params=pltpu.CompilerParams(vmem_limit_bytes=LIMIT),
        name="early",
    )(conv, inputs)
    *outs, residue = pl.pallas_call(
        functools.partial(second_kernel, shape),
        in_specs=[VMEM] * 7,
        out_specs=[HBM] * 5,
        out_shape=[big] * 4 + [jax.ShapeDtypeStruct((modes, channels), F32)],
        scratch_shapes=[
            pltpu.VMEM((shape.rows, LANES), F32),
            pltpu.VMEM((2, shape.halves, shape.length, BLOCK), BF16),
            pltpu.VMEM((modes * GROUPS, LANES), F32),
            pltpu.VMEM((modes, channels), F32),
            pltpu.SemaphoreType.DMA((2, copies)),
            pltpu.SemaphoreType.DMA((2, shape.halves)),
            pltpu.SemaphoreType.DMA((shape.halves,)),
        ],
        compiler_params=pltpu.CompilerParams(vmem_limit_bytes=LIMIT),
        name="second",
    )(early, wide, inputs, sent, table, scale, received)
    return outs, residue


def many(shape, arrays, rates, owners):
    modes, channels = shape.modes, shape.channels
    big = jax.ShapeDtypeStruct((shape.length, channels), BF16)
    copies = shape.halves * shape.chunks
    wide, inputs, ends, table, scale = pl.pallas_call(
        functools.partial(ends_kernel, shape),
        in_specs=[HBM] * 6,
        out_specs=[VMEM] * 5,
        out_shape=[
            pltpu.VMEM((2, shape.rows, LANES), F32),
            pltpu.VMEM((4, shape.halves, shape.length, BLOCK), BF16),
            jax.ShapeDtypeStruct((3, modes, shape.groups, LANES), F32),
            pltpu.VMEM((2 * modes * shape.groups, LANES), F32),
            jax.ShapeDtypeStruct((modes, channels), F32),
        ],
        scratch_shapes=[
            pltpu.VMEM((modes, channels), F32),
            pltpu.VMEM((modes, channels), F32),
            pltpu.SemaphoreType.DMA((4, copies)),
            pltpu.SemaphoreType.DMA((2,)),
        ],
        compiler_params=pltpu.CompilerParams(vmem_limit_bytes=LIMIT),
        name="ends",
    )(*arrays)
    rates = rates.reshape(modes, shape.groups, LANES)
    here = lax.axis_index("ctx")
    parts = lax.all_gather(ends[:2].astype(BF16), "ctx", axis=0).astype(F32)
    owner = jnp.arange(owners, dtype=jnp.int32)
    gaps = jnp.stack([here - 1 - owner, owner - 1 - here], axis=1).astype(F32)[:, :, None, None, None]
    decay = jnp.exp(-rates * shape.length * jnp.maximum(gaps, 0.0))
    starts = jnp.sum(jnp.where(gaps >= 0, decay, 0.0) * parts, axis=0)
    dots = ends[2] + jnp.exp(-rates) * ends[1] * starts[0]
    total = jnp.sum(lax.all_gather(dots.astype(BF16), "ctx", axis=0).astype(F32), axis=0)
    residue = total.reshape(modes, channels) * scale
    outs = pl.pallas_call(
        functools.partial(both_kernel, shape),
        in_specs=[VMEM] * 4,
        out_specs=[HBM] * 4,
        out_shape=[big] * 4,
        scratch_shapes=[
            pltpu.VMEM((shape.rows, LANES), F32),
            pltpu.VMEM((2, shape.halves, shape.length, BLOCK), BF16),
            pltpu.SemaphoreType.DMA((2, copies)),
        ],
        compiler_params=pltpu.CompilerParams(vmem_limit_bytes=LIMIT),
        name="both",
    )(wide, inputs, starts, table)
    return outs, residue


def body(owners, query_branch, key_branch, value_branch, output_grad, residues, decay_rates):
    length, channels = query_branch.shape
    rates = decay_rates.T
    shape = Shape(length, channels, rates.shape[0])
    hbm = functools.partial(pltpu.with_memory_space_constraint, memory_space=pltpu.HBM)
    arrays = [
        hbm(array)
        for array in (query_branch, output_grad, value_branch, key_branch, rates, residues.T)
    ]
    outs, residue = pair(shape, arrays) if owners == 2 else many(shape, arrays, rates, owners)
    mixed_out, query_grad, key_grad, value_grad = outs
    return (mixed_out, query_grad, key_grad, value_grad, residue.T)


def solution(mesh):
    tokens = P(("dp", "ctx"), "tp")
    return jax.shard_map(
        functools.partial(body, mesh.shape["ctx"]),
        mesh=mesh,
        in_specs=(tokens,) * 4 + (P("tp", None),) * 2,
        out_specs=(tokens,) * 4 + (P(("dp", "tp"), None),),
        check_vma=False,
    )
```

```python
import functools

import jax
import jax.numpy as jnp
from jax import lax
from jax.experimental import pallas as pl
from jax.experimental.pallas import tpu as pltpu
from jax.sharding import PartitionSpec as P

F32 = jnp.float32
BF16 = jnp.bfloat16
LANES = 128
GROUPS = 8
BLOCK = GROUPS * LANES
PAD = 8
UNROLL = 64


def one_minus_exp_2(rate, factor):
    square = rate * rate
    sinh = rate * (1.0 + square * (1 / 6 + square * (1 / 120 + square * (1 / 5040))))
    return 2.0 * factor * sinh


def mode_tables(rates, residues, table):
    modes, channels = rates.shape
    factor = jnp.exp(-rates)
    scale = jnp.sqrt(one_minus_exp_2(rates, factor) / modes)
    weight = residues * scale
    groups = channels // LANES
    for group in range(groups):
        lanes = slice(group * LANES, (group + 1) * LANES)
        table[pl.ds(group * modes, modes), :] = factor[:, lanes]
        table[pl.ds((groups + group) * modes, modes), :] = weight[:, lanes]
    return scale


def table_rows(table, which, half, modes, groups):
    start = (which * groups + half * GROUPS) * modes
    return [table[pl.ds(start + mode, GROUPS, stride=modes), :] for mode in range(modes)]


def tree_sum(terms):
    while len(terms) > 1:
        terms = [
            terms[i] + terms[i + 1] if i + 1 < len(terms) else terms[i]
            for i in range(0, len(terms), 2)
        ]
    return terms[0]


class Shape:
    def __init__(self, length, channels, modes):
        self.length = length
        self.channels = channels
        self.modes = modes
        self.halves = channels // BLOCK
        self.groups = channels // LANES
        self.chunk = min(64, length)
        self.chunks = length // self.chunk
        self.stride = length + PAD
        self.plane = GROUPS * self.stride
        self.rows = self.halves * self.plane


def lanes_of(half, group=None):
    if group is None:
        return pl.ds(pl.multiple_of(half * BLOCK, BLOCK), BLOCK)
    return pl.ds(pl.multiple_of(half * BLOCK + group * LANES, LANES), LANES)


def groups_of(half):
    return pl.ds(pl.multiple_of(half * GROUPS, GROUPS), GROUPS)


def products(shape, half, token, inputs, wide):
    step = min(32, shape.chunk)

    def body(i, carry):
        at = pl.multiple_of(token + i * step, step)
        for group in range(GROUPS):
            lane = slice(group * LANES, (group + 1) * LANES)
            row = half * shape.plane + group * shape.stride + at
            rows = pl.ds(pl.multiple_of(row, GROUPS), step)
            q, dy, v, k = [inputs[j, half, pl.ds(at, step), lane] for j in range(4)]
            wide[0, rows, :] = (k * v).astype(F32)
            wide[1, rows, :] = (dy * q).astype(F32)
        return carry

    lax.fori_loop(0, shape.chunk // step, body, 0)


def recurrence(shape, half, direction, chunk_index, factor, weight, state, dot, wide, conv):
    sign = 1 - 2 * direction
    begin = direction * (shape.length - 1) + sign * chunk_index * shape.chunk
    begin = half * shape.plane + begin
    steps = [sign * j for j in range(UNROLL)]
    stride = sign * UNROLL
    modes = shape.modes

    def body(i, carry):
        state, dot = list(carry[0]), list(carry[1])
        for j in range(UNROLL):
            rows = pl.ds(begin + i * stride + steps[j], GROUPS, stride=shape.stride)
            source = wide[direction, rows, :]
            other = wide[1 - direction, rows, :] if dot else None
            terms = []
            for mode in range(modes):
                state[mode] = factor[mode] * state[mode] + source
                if weight is not None:
                    terms.append(weight[mode] * state[mode])
                if dot:
                    dot[mode] = dot[mode] + other * state[mode]
            if weight is not None:
                conv[rows, :] = tree_sum(terms)
        return tuple(state), tuple(dot)

    state, dot = lax.fori_loop(0, shape.chunk // UNROLL, body, (tuple(state), tuple(dot)))
    return list(state), list(dot)


def outputs(shape, half, token, pair, inputs, conv, staged):
    step = min(32, shape.chunk)

    def body(i, carry):
        at = pl.multiple_of(token + i * step, step)
        for group in range(GROUPS):
            lane = slice(group * LANES, (group + 1) * LANES)
            row = half * shape.plane + group * shape.stride + at
            rows = pl.ds(pl.multiple_of(row, GROUPS), step)
            value = conv[rows, :]
            for j in range(2):
                staged[j, half, pl.ds(at, step), lane] = (
                    inputs[2 * pair + j, half, pl.ds(at, step), lane].astype(F32) * value
                ).astype(BF16)
        return carry

    lax.fori_loop(0, shape.chunk // step, body, 0)


def token_of(shape, direction, chunk_index):
    last = shape.chunks - 1
    return pl.multiple_of(
        (chunk_index + direction * (last - 2 * chunk_index)) * shape.chunk, shape.chunk
    )


def in_copy(shape, j, half, direction, chunk, source, inputs, sem):
    rows = pl.ds(token_of(shape, direction, chunk), shape.chunk)
    return pltpu.make_async_copy(
        source.at[rows, lanes_of(half)], inputs.at[j, half, rows, :], sem.at[half * shape.chunks + chunk]
    )


def in_wait(shape, half, direction, chunk, inputs, sem):
    landed = inputs.at[:, half, pl.ds(token_of(shape, direction, chunk), shape.chunk), :]
    pltpu.make_async_copy(landed, landed, sem.at[half * shape.chunks + chunk]).wait()


def out_copy(shape, j, half, direction, chunk, staged, target, sem):
    rows = pl.ds(token_of(shape, direction, chunk), shape.chunk)
    return pltpu.make_async_copy(
        staged.at[j, half, rows, :], target.at[rows, lanes_of(half)], sem
    )


def send_out(shape, half, pair, direction, chunk, staged, targets, sem):
    for p in range(2):

        @pl.when(pair == p)
        def _():
            for j in range(2):
                out_copy(shape, j, half, direction, chunk, staged, targets[2 * p + j], sem).start()


def wait_all(array, sem):
    pltpu.make_async_copy(array, array, sem).wait()


def start_coefficients(rates_hbm, res_hbm, coef, sem):
    pltpu.make_async_copy(rates_hbm, coef.at[0], sem).start()
    pltpu.make_async_copy(res_hbm, coef.at[1], sem).start()


def first_kernel(
    shape, q, dy, v, k, rates_hbm, res_hbm,
    conv, wide, inputs, sent, table, scale,
    coef, in_sem, coef_sem,
):
    direction = lax.axis_index("ctx")
    sources = (q, dy, v, k)
    start_coefficients(rates_hbm, res_hbm, coef, coef_sem)
    for half in range(shape.halves):
        for chunk in range(shape.chunks):
            for j in range(4):
                in_copy(shape, j, half, direction, chunk, sources[j], inputs, in_sem).start()
    wait_all(coef, coef_sem)
    scale[...] = mode_tables(coef[0], coef[1], table)
    zeros = (jnp.zeros((GROUPS, LANES), F32),) * shape.modes

    def sweep(half, _):
        factor = table_rows(table, 0, half, shape.modes, shape.groups)
        weight = table_rows(table, 1, half, shape.modes, shape.groups)

        def body(chunk, carry):
            token = token_of(shape, direction, chunk)
            in_wait(shape, half, direction, chunk, inputs, in_sem)
            products(shape, half, token, inputs, wide)
            state, dot = recurrence(
                shape, half, direction, chunk, factor, weight, carry[0], carry[1], wide, conv
            )
            return tuple(state), tuple(dot)

        state, dot = lax.fori_loop(0, shape.chunks, body, (zeros, zeros))
        for mode in range(shape.modes):
            sent[0, mode, groups_of(half), :] = state[mode].astype(BF16)
            sent[1, mode, groups_of(half), :] = dot[mode].astype(BF16)
        return 0

    lax.fori_loop(0, shape.halves, sweep, 0)


def early_kernel(shape, conv, inputs, staged):
    direction = lax.axis_index("ctx")

    def body(i, carry):
        half, chunk = i // shape.chunks, i % shape.chunks
        outputs(shape, half, token_of(shape, 0, chunk), direction, inputs, conv, staged)
        return carry

    lax.fori_loop(0, shape.halves * shape.chunks, body, 0)


def early_copy(j, half, early, target, sem):
    return pltpu.make_async_copy(
        early.at[j, half], target.at[:, lanes_of(half)], sem
    )


def second_kernel(
    shape, early, wide, inputs, sent, table, scale, received,
    out0, out1, out2, out3, residue,
    conv, staged, totals, total, out_sem, early_sem, residue_sem,
):
    owner = lax.axis_index("ctx")
    direction = 1 - owner
    targets = (out0, out1, out2, out3)
    modes = shape.modes
    for p in range(2):

        @pl.when(owner == p)
        def _():
            for j in range(2):
                for half in range(shape.halves):
                    early_copy(j, half, early, targets[2 * p + j], early_sem).start()

    def sweep(half, _):
        factor = table_rows(table, 0, half, modes, shape.groups)
        weight = table_rows(table, 1, half, modes, shape.groups)
        state = []
        for mode in range(modes):
            mine = sent[0, mode, groups_of(half), :].astype(F32)
            theirs = received[0, mode, groups_of(half), :].astype(F32)
            mine_dot = sent[1, mode, groups_of(half), :].astype(F32)
            their_dot = received[1, mode, groups_of(half), :].astype(F32)
            totals[pl.ds(mode * GROUPS, GROUPS), :] = (
                mine_dot + their_dot + factor[mode] * (mine * theirs)
            )
            state.append(theirs)
        for group in range(GROUPS):
            lane = lanes_of(half, group)
            total[:, lane] = totals[pl.ds(group, modes, stride=GROUPS), :] * scale[:, lane]
        lane = lanes_of(half)
        pltpu.make_async_copy(total.at[:, lane], residue.at[:, lane], residue_sem).start()

        def body(chunk, state):
            token = token_of(shape, direction, chunk)
            state, _ = recurrence(
                shape, half, direction, chunk, factor, weight, state, (), wide, conv
            )
            outputs(shape, half, token, direction, inputs, conv, staged)
            send_out(shape, half, direction, direction, chunk, staged, targets, out_sem)
            return tuple(state)

        lax.fori_loop(0, shape.chunks, body, tuple(state))
        return 0

    lax.fori_loop(0, shape.halves, sweep, 0)
    wait_all(early, early_sem)
    wait_all(total, residue_sem)
    wait_all(staged, out_sem)


def ends_kernel(
    shape, q, dy, v, k, rates_hbm, res_hbm,
    wide, inputs, ends, table, scale,
    coef, in_sem, coef_sem,
):
    sources = (q, dy, v, k)
    start_coefficients(rates_hbm, res_hbm, coef, coef_sem)
    for half in range(shape.halves):
        for chunk in range(shape.chunks):
            for j in range(4):
                in_copy(shape, j, half, 0, chunk, sources[j], inputs, in_sem).start()
    wait_all(coef, coef_sem)
    scale[...] = mode_tables(coef[0], coef[1], table)
    zeros = (jnp.zeros((GROUPS, LANES), F32),) * shape.modes
    for half in range(shape.halves):
        factor = table_rows(table, 0, half, shape.modes, shape.groups)

        def forward(chunk, carry):
            in_wait(shape, half, 0, chunk, inputs, in_sem)
            products(shape, half, token_of(shape, 0, chunk), inputs, wide)
            state, dot = recurrence(
                shape, half, 0, chunk, factor, None, carry[0], carry[1], wide, None
            )
            return tuple(state), tuple(dot)

        def backward(chunk, state):
            state, _ = recurrence(shape, half, 1, chunk, factor, None, state, (), wide, None)
            return tuple(state)

        state, dot = lax.fori_loop(0, shape.chunks, forward, (zeros, zeros))
        back = lax.fori_loop(0, shape.chunks, backward, zeros)
        rows = groups_of(half)
        for mode in range(shape.modes):
            ends[0, mode, rows, :] = state[mode]
            ends[1, mode, rows, :] = back[mode]
            ends[2, mode, rows, :] = dot[mode]


def both_kernel(
    shape, wide, inputs, starts, table,
    out0, out1, out2, out3,
    conv, staged, out_sem,
):
    targets = (out0, out1, out2, out3)
    for direction in range(2):
        for half in range(shape.halves):
            rows = groups_of(half)
            factor = table_rows(table, 0, half, shape.modes, shape.groups)
            weight = table_rows(table, 1, half, shape.modes, shape.groups)
            state = tuple(starts[direction, mode, rows, :] for mode in range(shape.modes))

            def body(chunk, state):
                token = token_of(shape, direction, chunk)
                state, _ = recurrence(
                    shape, half, direction, chunk, factor, weight, state, (), wide, conv
                )
                outputs(shape, half, token, direction, inputs, conv, staged)
                for j in range(2):
                    out_copy(
                        shape, j, half, direction, chunk, staged, targets[2 * direction + j], out_sem
                    ).start()
                return tuple(state)

            lax.fori_loop(0, shape.chunks, body, state)
        wait_all(staged, out_sem)


HBM = pl.BlockSpec(memory_space=pltpu.HBM)
VMEM = pl.BlockSpec(memory_space=pltpu.VMEM)
LIMIT = 24 << 20


def pair(shape, arrays):
    modes, channels = shape.modes, shape.channels
    big = jax.ShapeDtypeStruct((shape.length, channels), BF16)
    copies = shape.halves * shape.chunks
    conv, wide, inputs, sent, table, scale = pl.pallas_call(
        functools.partial(first_kernel, shape),
        in_specs=[HBM] * 6,
        out_specs=[VMEM] * 6,
        out_shape=[
            pltpu.VMEM((shape.rows, LANES), F32),
            pltpu.VMEM((2, shape.rows, LANES), F32),
            pltpu.VMEM((4, shape.halves, shape.length, BLOCK), BF16),
            jax.ShapeDtypeStruct((2, modes, shape.groups, LANES), BF16),
            pltpu.VMEM((2 * modes * shape.groups, LANES), F32),
            pltpu.VMEM((modes, channels), F32),
        ],
        scratch_shapes=[
            pltpu.VMEM((2, modes, channels), F32),
            pltpu.SemaphoreType.DMA((copies,)),
            pltpu.SemaphoreType.DMA,
        ],
        compiler_params=pltpu.CompilerParams(vmem_limit_bytes=LIMIT),
        name="first",
    )(*arrays)
    received = lax.ppermute(sent, "ctx", [(0, 1), (1, 0)])
    early = pl.pallas_call(
        functools.partial(early_kernel, shape),
        in_specs=[VMEM] * 2,
        out_specs=VMEM,
        out_shape=pltpu.VMEM((2, shape.halves, shape.length, BLOCK), BF16),
        compiler_params=pltpu.CompilerParams(vmem_limit_bytes=LIMIT),
        name="early",
    )(conv, inputs)
    *outs, residue = pl.pallas_call(
        functools.partial(second_kernel, shape),
        in_specs=[VMEM] * 7,
        out_specs=[HBM] * 5,
        out_shape=[big] * 4 + [jax.ShapeDtypeStruct((modes, channels), F32)],
        scratch_shapes=[
            pltpu.VMEM((shape.rows, LANES), F32),
            pltpu.VMEM((2, shape.halves, shape.length, BLOCK), BF16),
            pltpu.VMEM((modes * GROUPS, LANES), F32),
            pltpu.VMEM((modes, channels), F32),
            pltpu.SemaphoreType.DMA,
            pltpu.SemaphoreType.DMA,
            pltpu.SemaphoreType.DMA,
        ],
        compiler_params=pltpu.CompilerParams(vmem_limit_bytes=LIMIT),
        name="second",
    )(early, wide, inputs, sent, table, scale, received)
    return outs, residue


def many(shape, arrays, rates, owners):
    modes, channels = shape.modes, shape.channels
    big = jax.ShapeDtypeStruct((shape.length, channels), BF16)
    copies = shape.halves * shape.chunks
    wide, inputs, ends, table, scale = pl.pallas_call(
        functools.partial(ends_kernel, shape),
        in_specs=[HBM] * 6,
        out_specs=[VMEM] * 5,
        out_shape=[
            pltpu.VMEM((2, shape.rows, LANES), F32),
            pltpu.VMEM((4, shape.halves, shape.length, BLOCK), BF16),
            jax.ShapeDtypeStruct((3, modes, shape.groups, LANES), F32),
            pltpu.VMEM((2 * modes * shape.groups, LANES), F32),
            jax.ShapeDtypeStruct((modes, channels), F32),
        ],
        scratch_shapes=[
            pltpu.VMEM((2, modes, channels), F32),
            pltpu.SemaphoreType.DMA((copies,)),
            pltpu.SemaphoreType.DMA,
        ],
        compiler_params=pltpu.CompilerParams(vmem_limit_bytes=LIMIT),
        name="ends",
    )(*arrays)
    rates = rates.reshape(modes, shape.groups, LANES)
    here = lax.axis_index("ctx")
    parts = lax.all_gather(ends[:2].astype(BF16), "ctx", axis=0).astype(F32)
    owner = jnp.arange(owners, dtype=jnp.int32)
    gaps = jnp.stack([here - 1 - owner, owner - 1 - here], axis=1).astype(F32)[:, :, None, None, None]
    decay = jnp.exp(-rates * shape.length * jnp.maximum(gaps, 0.0))
    starts = jnp.sum(jnp.where(gaps >= 0, decay, 0.0) * parts, axis=0)
    dots = ends[2] + jnp.exp(-rates) * ends[1] * starts[0]
    total = jnp.sum(lax.all_gather(dots.astype(BF16), "ctx", axis=0).astype(F32), axis=0)
    residue = total.reshape(modes, channels) * scale
    outs = pl.pallas_call(
        functools.partial(both_kernel, shape),
        in_specs=[VMEM] * 4,
        out_specs=[HBM] * 4,
        out_shape=[big] * 4,
        scratch_shapes=[
            pltpu.VMEM((shape.rows, LANES), F32),
            pltpu.VMEM((2, shape.halves, shape.length, BLOCK), BF16),
            pltpu.SemaphoreType.DMA,
        ],
        compiler_params=pltpu.CompilerParams(vmem_limit_bytes=LIMIT),
        name="both",
    )(wide, inputs, starts, table)
    return outs, residue


def body(owners, query_branch, key_branch, value_branch, output_grad, residues, decay_rates):
    length, channels = query_branch.shape
    rates = decay_rates.T
    shape = Shape(length, channels, rates.shape[0])
    hbm = functools.partial(pltpu.with_memory_space_constraint, memory_space=pltpu.HBM)
    arrays = [
        hbm(array)
        for array in (query_branch, output_grad, value_branch, key_branch, rates, residues.T)
    ]
    outs, residue = pair(shape, arrays) if owners == 2 else many(shape, arrays, rates, owners)
    mixed_out, query_grad, key_grad, value_grad = outs
    return (mixed_out, query_grad, key_grad, value_grad, residue.T)


def solution(mesh):
    tokens = P(("dp", "ctx"), "tp")
    return jax.shard_map(
        functools.partial(body, mesh.shape["ctx"]),
        mesh=mesh,
        in_specs=(tokens,) * 4 + (P("tp", None),) * 2,
        out_specs=(tokens,) * 4 + (P(("dp", "tp"), None),),
        check_vma=False,
    )
```

```python
import functools

import jax
import jax.numpy as jnp
from jax import lax
from jax.experimental import pallas as pl
from jax.experimental.pallas import tpu as pltpu
from jax.sharding import PartitionSpec as P

F32 = jnp.float32
BF16 = jnp.bfloat16
LANES = 128
GROUPS = 8
BLOCK = GROUPS * LANES
PAD = 8
UNROLL = 64


def one_minus_exp_2(rate, factor):
    square = rate * rate
    sinh = rate * (1.0 + square * (1 / 6 + square * (1 / 120 + square * (1 / 5040))))
    return 2.0 * factor * sinh


def mode_tables(rates, residues, table):
    modes, channels = rates.shape
    factor = jnp.exp(-rates)
    scale = jnp.sqrt(one_minus_exp_2(rates, factor) / modes)
    weight = residues * scale
    groups = channels // LANES
    for group in range(groups):
        lanes = slice(group * LANES, (group + 1) * LANES)
        table[pl.ds(group * modes, modes), :] = factor[:, lanes]
        table[pl.ds((groups + group) * modes, modes), :] = weight[:, lanes]
    return scale


def table_rows(table, which, half, modes, groups):
    start = (which * groups + half * GROUPS) * modes
    return [table[pl.ds(start + mode, GROUPS, stride=modes), :] for mode in range(modes)]


def tree_sum(terms):
    while len(terms) > 1:
        terms = [
            terms[i] + terms[i + 1] if i + 1 < len(terms) else terms[i]
            for i in range(0, len(terms), 2)
        ]
    return terms[0]


class Shape:
    def __init__(self, length, channels, modes):
        self.length = length
        self.channels = channels
        self.modes = modes
        self.halves = channels // BLOCK
        self.groups = channels // LANES
        self.chunk = min(64, length)
        self.chunks = length // self.chunk
        self.stride = length + PAD
        self.plane = GROUPS * self.stride
        self.rows = self.halves * self.plane


def lanes_of(half, group=None):
    if group is None:
        return pl.ds(pl.multiple_of(half * BLOCK, BLOCK), BLOCK)
    return pl.ds(pl.multiple_of(half * BLOCK + group * LANES, LANES), LANES)


def groups_of(half):
    return pl.ds(pl.multiple_of(half * GROUPS, GROUPS), GROUPS)


def products(shape, half, token, inputs, wide):
    step = min(32, shape.chunk)

    def body(i, carry):
        at = pl.multiple_of(token + i * step, step)
        for group in range(GROUPS):
            lane = slice(group * LANES, (group + 1) * LANES)
            row = half * shape.plane + group * shape.stride + at
            rows = pl.ds(pl.multiple_of(row, GROUPS), step)
            q, dy, v, k = [inputs[j, half, pl.ds(at, step), lane] for j in range(4)]
            wide[0, rows, :] = (k * v).astype(F32)
            wide[1, rows, :] = (dy * q).astype(F32)
        return carry

    lax.fori_loop(0, shape.chunk // step, body, 0)


def recurrence(shape, half, direction, chunk_index, factor, weight, state, dot, wide, conv):
    sign = 1 - 2 * direction
    begin = direction * (shape.length - 1) + sign * chunk_index * shape.chunk
    begin = half * shape.plane + begin
    steps = [sign * j for j in range(UNROLL)]
    stride = sign * UNROLL
    modes = shape.modes

    def body(i, carry):
        state, dot = list(carry[0]), list(carry[1])
        for j in range(UNROLL):
            rows = pl.ds(begin + i * stride + steps[j], GROUPS, stride=shape.stride)
            source = wide[direction, rows, :]
            other = wide[1 - direction, rows, :] if dot else None
            terms = []
            for mode in range(modes):
                state[mode] = factor[mode] * state[mode] + source
                if weight is not None:
                    terms.append(weight[mode] * state[mode])
                if dot:
                    dot[mode] = dot[mode] + other * state[mode]
            if weight is not None:
                conv[rows, :] = tree_sum(terms)
        return tuple(state), tuple(dot)

    state, dot = lax.fori_loop(0, shape.chunk // UNROLL, body, (tuple(state), tuple(dot)))
    return list(state), list(dot)


def rows_of(shape, half, direction, chunk):
    sign = 1 - 2 * direction
    begin = half * shape.plane + direction * (shape.length - 1) + sign * chunk * shape.chunk
    return lambda j: pl.ds(begin + sign * j, GROUPS, stride=shape.stride)


def pair_rows(shape, half, pair, slot):
    row = ((half * (shape.length // 2) + pair) * (shape.modes + 1) + slot) * GROUPS
    return pl.ds(pl.multiple_of(row, GROUPS), GROUPS)


def first_sweep(shape, half, direction, chunk, factor, weight, state, dot, rest, wide, conv, ahead):
    rows_at = rows_of(shape, half, direction, chunk)
    modes = shape.modes
    state, dot = list(state), list(dot)
    for j in range(0, shape.chunk, 2):
        pair = chunk * (shape.chunk // 2) + j // 2
        rows0, rows1 = rows_at(j), rows_at(j + 1)
        source0, source1 = wide[direction, rows0, :], wide[direction, rows1, :]
        other0, other1 = wide[1 - direction, rows0, :], wide[1 - direction, rows1, :]
        state = [factor[mode] * state[mode] + source0 for mode in range(modes)]
        conv[rows0, :] = tree_sum([weight[mode] * state[mode] for mode in range(modes)])
        for mode in range(modes):
            both = other0 + factor[mode] * other1
            ahead[pair_rows(shape, half, pair, mode), :] = both
            dot[mode] = dot[mode] + state[mode] * both
        rest = rest + source1 * other1
        ahead[pair_rows(shape, half, pair, modes), :] = other1
        state = [factor[mode] * state[mode] + source1 for mode in range(modes)]
        conv[rows1, :] = tree_sum([weight[mode] * state[mode] for mode in range(modes)])
    return tuple(state), tuple(dot), rest


def second_sweep(shape, half, direction, chunk, square, weight, weight_next, now, state, ahead, conv):
    rows_at = rows_of(shape, half, direction, chunk)
    modes = shape.modes
    state = list(state)
    for j in range(0, shape.chunk, 2):
        pair = shape.length // 2 - 1 - chunk * (shape.chunk // 2) - j // 2
        terms = [weight_next[mode] * state[mode] for mode in range(modes)]
        terms.append(now * ahead[pair_rows(shape, half, pair, modes), :])
        conv[rows_at(j), :] = tree_sum(terms)
        state = [
            square[mode] * state[mode] + ahead[pair_rows(shape, half, pair, mode), :]
            for mode in range(modes)
        ]
        conv[rows_at(j + 1), :] = tree_sum([weight[mode] * state[mode] for mode in range(modes)])
    return tuple(state)


def outputs(shape, half, token, pair, inputs, conv, staged):
    step = min(32, shape.chunk)

    def body(i, carry):
        at = pl.multiple_of(token + i * step, step)
        for group in range(GROUPS):
            lane = slice(group * LANES, (group + 1) * LANES)
            row = half * shape.plane + group * shape.stride + at
            rows = pl.ds(pl.multiple_of(row, GROUPS), step)
            value = conv[rows, :]
            for j in range(2):
                staged[j, half, pl.ds(at, step), lane] = (
                    inputs[2 * pair + j, half, pl.ds(at, step), lane].astype(F32) * value
                ).astype(BF16)
        return carry

    lax.fori_loop(0, shape.chunk // step, body, 0)


def token_of(shape, direction, chunk_index):
    last = shape.chunks - 1
    return pl.multiple_of(
        (chunk_index + direction * (last - 2 * chunk_index)) * shape.chunk, shape.chunk
    )


def in_copy(shape, j, half, direction, chunk, source, inputs, sem):
    rows = pl.ds(token_of(shape, direction, chunk), shape.chunk)
    return pltpu.make_async_copy(
        source.at[rows, lanes_of(half)], inputs.at[j, half, rows, :], sem.at[half * shape.chunks + chunk]
    )


def in_wait(shape, half, direction, chunk, inputs, sem):
    landed = inputs.at[:, half, pl.ds(token_of(shape, direction, chunk), shape.chunk), :]
    pltpu.make_async_copy(landed, landed, sem.at[half * shape.chunks + chunk]).wait()


def out_copy(shape, j, half, direction, chunk, staged, target, sem):
    rows = pl.ds(token_of(shape, direction, chunk), shape.chunk)
    return pltpu.make_async_copy(
        staged.at[j, half, rows, :], target.at[rows, lanes_of(half)], sem
    )


def send_out(shape, half, pair, direction, chunk, staged, targets, sem):
    for p in range(2):

        @pl.when(pair == p)
        def _():
            for j in range(2):
                out_copy(shape, j, half, direction, chunk, staged, targets[2 * p + j], sem).start()


def wait_all(array, sem):
    pltpu.make_async_copy(array, array, sem).wait()


def start_coefficients(rates_hbm, res_hbm, coef, sem):
    pltpu.make_async_copy(rates_hbm, coef.at[0], sem).start()
    pltpu.make_async_copy(res_hbm, coef.at[1], sem).start()


def first_kernel(
    shape, q, dy, v, k, rates_hbm, res_hbm,
    conv, ahead, inputs, sent, table, scale,
    wide, coef, in_sem, coef_sem,
):
    direction = lax.axis_index("ctx")
    sources = (q, dy, v, k)
    start_coefficients(rates_hbm, res_hbm, coef, coef_sem)
    for half in range(shape.halves):
        for chunk in range(shape.chunks):
            for j in range(4):
                in_copy(shape, j, half, direction, chunk, sources[j], inputs, in_sem).start()
    wait_all(coef, coef_sem)
    scale[...] = mode_tables(coef[0], coef[1], table)
    zeros = (jnp.zeros((GROUPS, LANES), F32),) * shape.modes

    def run(way):
        def sweep(half, _):
            factor = table_rows(table, 0, half, shape.modes, shape.groups)
            weight = table_rows(table, 1, half, shape.modes, shape.groups)

            def body(chunk, carry):
                token = token_of(shape, way, chunk)
                in_wait(shape, half, way, chunk, inputs, in_sem)
                products(shape, half, token, inputs, wide)
                return first_sweep(
                    shape, half, way, chunk, factor, weight, *carry, wide, conv, ahead
                )

            state, dot, rest = lax.fori_loop(0, shape.chunks, body, (zeros, zeros, zeros[0]))
            for mode in range(shape.modes):
                sent[0, mode, groups_of(half), :] = state[mode].astype(BF16)
                sent[1, mode, groups_of(half), :] = (dot[mode] + rest).astype(BF16)
            return 0

        lax.fori_loop(0, shape.halves, sweep, 0)

    for way in range(2):
        pl.when(direction == way)(functools.partial(run, way))


def early_kernel(shape, conv, inputs, staged):
    direction = lax.axis_index("ctx")

    def body(i, carry):
        half, chunk = i // shape.chunks, i % shape.chunks
        outputs(shape, half, token_of(shape, 0, chunk), direction, inputs, conv, staged)
        return carry

    lax.fori_loop(0, shape.halves * shape.chunks, body, 0)


def early_copy(j, half, early, target, sem):
    return pltpu.make_async_copy(
        early.at[j, half], target.at[:, lanes_of(half)], sem
    )


def second_kernel(
    shape, early, ahead, inputs, sent, table, scale, received,
    out0, out1, out2, out3, residue,
    conv, staged, totals, total, out_sem, early_sem, residue_sem,
):
    owner = lax.axis_index("ctx")
    direction = 1 - owner
    targets = (out0, out1, out2, out3)
    modes = shape.modes
    for p in range(2):

        @pl.when(owner == p)
        def _():
            for j in range(2):
                for half in range(shape.halves):
                    early_copy(j, half, early, targets[2 * p + j], early_sem).start()

    def run(way):
        def sweep(half, _):
            factor = table_rows(table, 0, half, modes, shape.groups)
            weight = table_rows(table, 1, half, modes, shape.groups)
            square = [value * value for value in factor]
            weight_next = [weight[mode] * factor[mode] for mode in range(modes)]
            now = tree_sum(weight)
            state = []
            for mode in range(modes):
                mine = sent[0, mode, groups_of(half), :].astype(F32)
                theirs = received[0, mode, groups_of(half), :].astype(F32)
                mine_dot = sent[1, mode, groups_of(half), :].astype(F32)
                their_dot = received[1, mode, groups_of(half), :].astype(F32)
                totals[pl.ds(mode * GROUPS, GROUPS), :] = (
                    mine_dot + their_dot + factor[mode] * (mine * theirs)
                )
                state.append(theirs)
            for group in range(GROUPS):
                lane = lanes_of(half, group)
                total[:, lane] = totals[pl.ds(group, modes, stride=GROUPS), :] * scale[:, lane]
            lane = lanes_of(half)
            pltpu.make_async_copy(total.at[:, lane], residue.at[:, lane], residue_sem).start()

            def body(chunk, state):
                token = token_of(shape, way, chunk)
                state = second_sweep(
                    shape, half, way, chunk, square, weight, weight_next, now, state, ahead, conv
                )
                outputs(shape, half, token, way, inputs, conv, staged)
                for j in range(2):
                    out_copy(
                        shape, j, half, way, chunk, staged, targets[2 * way + j], out_sem
                    ).start()
                return state

            lax.fori_loop(0, shape.chunks, body, tuple(state))
            return 0

        lax.fori_loop(0, shape.halves, sweep, 0)

    for way in range(2):
        pl.when(direction == way)(functools.partial(run, way))

    wait_all(early, early_sem)
    wait_all(total, residue_sem)
    wait_all(staged, out_sem)


def ends_kernel(
    shape, q, dy, v, k, rates_hbm, res_hbm,
    wide, inputs, ends, table, scale,
    coef, in_sem, coef_sem,
):
    sources = (q, dy, v, k)
    start_coefficients(rates_hbm, res_hbm, coef, coef_sem)
    for half in range(shape.halves):
        for chunk in range(shape.chunks):
            for j in range(4):
                in_copy(shape, j, half, 0, chunk, sources[j], inputs, in_sem).start()
    wait_all(coef, coef_sem)
    scale[...] = mode_tables(coef[0], coef[1], table)
    zeros = (jnp.zeros((GROUPS, LANES), F32),) * shape.modes
    for half in range(shape.halves):
        factor = table_rows(table, 0, half, shape.modes, shape.groups)

        def forward(chunk, carry):
            in_wait(shape, half, 0, chunk, inputs, in_sem)
            products(shape, half, token_of(shape, 0, chunk), inputs, wide)
            state, dot = recurrence(
                shape, half, 0, chunk, factor, None, carry[0], carry[1], wide, None
            )
            return tuple(state), tuple(dot)

        def backward(chunk, state):
            state, _ = recurrence(shape, half, 1, chunk, factor, None, state, (), wide, None)
            return tuple(state)

        state, dot = lax.fori_loop(0, shape.chunks, forward, (zeros, zeros))
        back = lax.fori_loop(0, shape.chunks, backward, zeros)
        rows = groups_of(half)
        for mode in range(shape.modes):
            ends[0, mode, rows, :] = state[mode]
            ends[1, mode, rows, :] = back[mode]
            ends[2, mode, rows, :] = dot[mode]


def both_kernel(
    shape, wide, inputs, starts, table,
    out0, out1, out2, out3,
    conv, staged, out_sem,
):
    targets = (out0, out1, out2, out3)
    for direction in range(2):
        for half in range(shape.halves):
            rows = groups_of(half)
            factor = table_rows(table, 0, half, shape.modes, shape.groups)
            weight = table_rows(table, 1, half, shape.modes, shape.groups)
            state = tuple(starts[direction, mode, rows, :] for mode in range(shape.modes))

            def body(chunk, state):
                token = token_of(shape, direction, chunk)
                state, _ = recurrence(
                    shape, half, direction, chunk, factor, weight, state, (), wide, conv
                )
                outputs(shape, half, token, direction, inputs, conv, staged)
                for j in range(2):
                    out_copy(
                        shape, j, half, direction, chunk, staged, targets[2 * direction + j], out_sem
                    ).start()
                return tuple(state)

            lax.fori_loop(0, shape.chunks, body, state)
        wait_all(staged, out_sem)


HBM = pl.BlockSpec(memory_space=pltpu.HBM)
VMEM = pl.BlockSpec(memory_space=pltpu.VMEM)
LIMIT = 24 << 20


def pair(shape, arrays):
    modes, channels = shape.modes, shape.channels
    big = jax.ShapeDtypeStruct((shape.length, channels), BF16)
    copies = shape.halves * shape.chunks
    conv, ahead, inputs, sent, table, scale = pl.pallas_call(
        functools.partial(first_kernel, shape),
        in_specs=[HBM] * 6,
        out_specs=[VMEM] * 6,
        out_shape=[
            pltpu.VMEM((shape.rows, LANES), F32),
            pltpu.VMEM((shape.groups * shape.length // 2 * (modes + 1), LANES), F32),
            pltpu.VMEM((4, shape.halves, shape.length, BLOCK), BF16),
            jax.ShapeDtypeStruct((2, modes, shape.groups, LANES), BF16),
            pltpu.VMEM((2 * modes * shape.groups, LANES), F32),
            pltpu.VMEM((modes, channels), F32),
        ],
        scratch_shapes=[
            pltpu.VMEM((2, shape.rows, LANES), F32),
            pltpu.VMEM((2, modes, channels), F32),
            pltpu.SemaphoreType.DMA((copies,)),
            pltpu.SemaphoreType.DMA,
        ],
        compiler_params=pltpu.CompilerParams(vmem_limit_bytes=LIMIT),
        name="first",
    )(*arrays)
    received = lax.ppermute(sent, "ctx", [(0, 1), (1, 0)])
    early = pl.pallas_call(
        functools.partial(early_kernel, shape),
        in_specs=[VMEM] * 2,
        out_specs=VMEM,
        out_shape=pltpu.VMEM((2, shape.halves, shape.length, BLOCK), BF16),
        compiler_params=pltpu.CompilerParams(vmem_limit_bytes=LIMIT),
        name="early",
    )(conv, inputs)
    *outs, residue = pl.pallas_call(
        functools.partial(second_kernel, shape),
        in_specs=[VMEM] * 7,
        out_specs=[HBM] * 5,
        out_shape=[big] * 4 + [jax.ShapeDtypeStruct((modes, channels), F32)],
        scratch_shapes=[
            pltpu.VMEM((shape.rows, LANES), F32),
            pltpu.VMEM((2, shape.halves, shape.length, BLOCK), BF16),
            pltpu.VMEM((modes * GROUPS, LANES), F32),
            pltpu.VMEM((modes, channels), F32),
            pltpu.SemaphoreType.DMA,
            pltpu.SemaphoreType.DMA,
            pltpu.SemaphoreType.DMA,
        ],
        compiler_params=pltpu.CompilerParams(vmem_limit_bytes=LIMIT),
        name="second",
    )(early, ahead, inputs, sent, table, scale, received)
    return outs, residue


def many(shape, arrays, rates, owners):
    modes, channels = shape.modes, shape.channels
    big = jax.ShapeDtypeStruct((shape.length, channels), BF16)
    copies = shape.halves * shape.chunks
    wide, inputs, ends, table, scale = pl.pallas_call(
        functools.partial(ends_kernel, shape),
        in_specs=[HBM] * 6,
        out_specs=[VMEM] * 5,
        out_shape=[
            pltpu.VMEM((2, shape.rows, LANES), F32),
            pltpu.VMEM((4, shape.halves, shape.length, BLOCK), BF16),
            jax.ShapeDtypeStruct((3, modes, shape.groups, LANES), F32),
            pltpu.VMEM((2 * modes * shape.groups, LANES), F32),
            jax.ShapeDtypeStruct((modes, channels), F32),
        ],
        scratch_shapes=[
            pltpu.VMEM((2, modes, channels), F32),
            pltpu.SemaphoreType.DMA((copies,)),
            pltpu.SemaphoreType.DMA,
        ],
        compiler_params=pltpu.CompilerParams(vmem_limit_bytes=LIMIT),
        name="ends",
    )(*arrays)
    rates = rates.reshape(modes, shape.groups, LANES)
    here = lax.axis_index("ctx")
    parts = lax.all_gather(ends[:2].astype(BF16), "ctx", axis=0).astype(F32)
    owner = jnp.arange(owners, dtype=jnp.int32)
    gaps = jnp.stack([here - 1 - owner, owner - 1 - here], axis=1).astype(F32)[:, :, None, None, None]
    decay = jnp.exp(-rates * shape.length * jnp.maximum(gaps, 0.0))
    starts = jnp.sum(jnp.where(gaps >= 0, decay, 0.0) * parts, axis=0)
    dots = ends[2] + jnp.exp(-rates) * ends[1] * starts[0]
    total = jnp.sum(lax.all_gather(dots.astype(BF16), "ctx", axis=0).astype(F32), axis=0)
    residue = total.reshape(modes, channels) * scale
    outs = pl.pallas_call(
        functools.partial(both_kernel, shape),
        in_specs=[VMEM] * 4,
        out_specs=[HBM] * 4,
        out_shape=[big] * 4,
        scratch_shapes=[
            pltpu.VMEM((shape.rows, LANES), F32),
            pltpu.VMEM((2, shape.halves, shape.length, BLOCK), BF16),
            pltpu.SemaphoreType.DMA,
        ],
        compiler_params=pltpu.CompilerParams(vmem_limit_bytes=LIMIT),
        name="both",
    )(wide, inputs, starts, table)
    return outs, residue


def body(owners, query_branch, key_branch, value_branch, output_grad, residues, decay_rates):
    length, channels = query_branch.shape
    rates = decay_rates.T
    shape = Shape(length, channels, rates.shape[0])
    hbm = functools.partial(pltpu.with_memory_space_constraint, memory_space=pltpu.HBM)
    arrays = [
        hbm(array)
        for array in (query_branch, output_grad, value_branch, key_branch, rates, residues.T)
    ]
    outs, residue = pair(shape, arrays) if owners == 2 else many(shape, arrays, rates, owners)
    mixed_out, query_grad, key_grad, value_grad = outs
    return (mixed_out, query_grad, key_grad, value_grad, residue.T)


def solution(mesh):
    tokens = P(("dp", "ctx"), "tp")
    return jax.shard_map(
        functools.partial(body, mesh.shape["ctx"]),
        mesh=mesh,
        in_specs=(tokens,) * 4 + (P("tp", None),) * 2,
        out_specs=(tokens,) * 4 + (P(("dp", "tp"), None),),
        check_vma=False,
    )
```

```python
import functools

import jax
import jax.numpy as jnp
from jax import lax
from jax.experimental import pallas as pl
from jax.experimental.pallas import tpu as pltpu
from jax.sharding import PartitionSpec as P

F32 = jnp.float32
BF16 = jnp.bfloat16
LANES = 128
GROUPS = 8
BLOCK = GROUPS * LANES
PAD = 8
UNROLL = 64


def one_minus_exp_2(rate, factor):
    square = rate * rate
    sinh = rate * (1.0 + square * (1 / 6 + square * (1 / 120 + square * (1 / 5040))))
    return 2.0 * factor * sinh


def mode_tables(rates, residues, table):
    modes, channels = rates.shape
    factor = jnp.exp(-rates)
    scale = jnp.sqrt(one_minus_exp_2(rates, factor) / modes)
    weight = residues * scale
    groups = channels // LANES
    for group in range(groups):
        lanes = slice(group * LANES, (group + 1) * LANES)
        table[pl.ds(group * modes, modes), :] = factor[:, lanes]
        table[pl.ds((groups + group) * modes, modes), :] = weight[:, lanes]
    return scale


def table_rows(table, which, half, modes, groups):
    start = (which * groups + half * GROUPS) * modes
    return [table[pl.ds(start + mode, GROUPS, stride=modes), :] for mode in range(modes)]


def tree_sum(terms):
    while len(terms) > 1:
        terms = [
            terms[i] + terms[i + 1] if i + 1 < len(terms) else terms[i]
            for i in range(0, len(terms), 2)
        ]
    return terms[0]


class Shape:
    def __init__(self, length, channels, modes):
        self.length = length
        self.channels = channels
        self.modes = modes
        self.halves = channels // BLOCK
        self.groups = channels // LANES
        self.chunk = min(64, length)
        self.chunks = length // self.chunk
        self.stride = length + PAD
        self.plane = GROUPS * self.stride
        self.rows = self.halves * self.plane


def lanes_of(half, group=None):
    if group is None:
        return pl.ds(pl.multiple_of(half * BLOCK, BLOCK), BLOCK)
    return pl.ds(pl.multiple_of(half * BLOCK + group * LANES, LANES), LANES)


def groups_of(half):
    return pl.ds(pl.multiple_of(half * GROUPS, GROUPS), GROUPS)


def products(shape, half, token, inputs, wide):
    step = min(32, shape.chunk)

    def body(i, carry):
        at = pl.multiple_of(token + i * step, step)
        for group in range(GROUPS):
            lane = slice(group * LANES, (group + 1) * LANES)
            row = half * shape.plane + group * shape.stride + at
            rows = pl.ds(pl.multiple_of(row, GROUPS), step)
            q, dy, v, k = [inputs[j, half, pl.ds(at, step), lane] for j in range(4)]
            wide[0, rows, :] = (k * v).astype(F32)
            wide[1, rows, :] = (dy * q).astype(F32)
        return carry

    lax.fori_loop(0, shape.chunk // step, body, 0)


def recurrence(shape, half, direction, chunk_index, factor, weight, state, dot, wide, conv):
    sign = 1 - 2 * direction
    begin = direction * (shape.length - 1) + sign * chunk_index * shape.chunk
    begin = half * shape.plane + begin
    steps = [sign * j for j in range(UNROLL)]
    stride = sign * UNROLL
    modes = shape.modes

    def body(i, carry):
        state, dot = list(carry[0]), list(carry[1])
        for j in range(UNROLL):
            rows = pl.ds(begin + i * stride + steps[j], GROUPS, stride=shape.stride)
            source = wide[direction, rows, :]
            other = wide[1 - direction, rows, :] if dot else None
            terms = []
            for mode in range(modes):
                state[mode] = factor[mode] * state[mode] + source
                if weight is not None:
                    terms.append(weight[mode] * state[mode])
                if dot:
                    dot[mode] = dot[mode] + other * state[mode]
            if weight is not None:
                conv[rows, :] = tree_sum(terms)
        return tuple(state), tuple(dot)

    state, dot = lax.fori_loop(0, shape.chunk // UNROLL, body, (tuple(state), tuple(dot)))
    return list(state), list(dot)


def rows_of(shape, half, direction, chunk):
    sign = 1 - 2 * direction
    begin = half * shape.plane + direction * (shape.length - 1) + sign * chunk * shape.chunk
    return lambda j: pl.ds(begin + sign * j, GROUPS, stride=shape.stride)


def pair_rows(shape, half, pair, slot):
    row = ((half * (shape.length // 2) + pair) * (shape.modes + 1) + slot) * GROUPS
    return pl.ds(pl.multiple_of(row, GROUPS), GROUPS)


def held_rows(shape, half, j, mode):
    row = ((half * shape.chunk + j) * shape.modes + mode) * GROUPS
    return pl.ds(pl.multiple_of(row, GROUPS), GROUPS)


def near_products(shape, half, direction, chunk, index, inputs, near):
    start = shape.chunk - 8 - 8 * index if direction else 8 * index
    at = pl.multiple_of(token_of(shape, direction, chunk) + start, 8)
    first, second = 2 * (1 - direction), 2 * direction
    for group in range(GROUPS):
        lane = slice(group * LANES, (group + 1) * LANES)
        rows = pl.ds(group * (shape.chunk + PAD) + start, 8)
        a0, a1, b0, b1 = [
            inputs[plane + j, half, pl.ds(at, 8), lane] for plane in (first, second) for j in range(2)
        ]
        near[0, rows, :] = (a0 * a1).astype(F32)
        near[1, rows, :] = (b0 * b1).astype(F32)


def first_sweep(
    shape, half, direction, chunk, coming, factor, weight, state, dot, rest,
    inputs, near, conv, ahead, held,
):
    rows_at = rows_of(shape, half, direction, chunk)
    modes = shape.modes
    state, dot = list(state), list(dot)

    def emit(j, state):
        if weight is not None:
            conv[rows_at(j), :] = tree_sum([weight[mode] * state[mode] for mode in range(modes)])
            return
        for mode in range(modes):
            held[held_rows(shape, half, j, mode), :] = state[mode]

    def near_row(j):
        token = shape.chunk - 1 - j if direction else j
        return pl.ds(token, GROUPS, stride=shape.chunk + PAD)

    for j in range(0, shape.chunk, 2):
        if j % 8 == 0:
            index = j // 8 + 1
            if index < shape.chunk // 8:
                near_products(shape, half, direction, chunk, index, inputs, near)
        pair = chunk * (shape.chunk // 2) + j // 2
        source0, source1 = near[0, near_row(j), :], near[0, near_row(j + 1), :]
        other0, other1 = near[1, near_row(j), :], near[1, near_row(j + 1), :]
        state = [factor[mode] * state[mode] + source0 for mode in range(modes)]
        emit(j, state)
        for mode in range(modes):
            both = other0 + factor[mode] * other1
            ahead[pair_rows(shape, half, pair, mode), :] = both
            dot[mode] = dot[mode] + state[mode] * both
        rest = rest + source1 * other1
        ahead[pair_rows(shape, half, pair, modes), :] = other1
        state = [factor[mode] * state[mode] + source1 for mode in range(modes)]
        emit(j + 1, state)
    near_products(shape, *coming, inputs, near)
    return tuple(state), tuple(dot), rest


def second_sweep(shape, half, direction, chunk, square, weight, weight_next, now, state, ahead, conv):
    rows_at = rows_of(shape, half, direction, chunk)
    modes = shape.modes
    state = list(state)
    for j in range(0, shape.chunk, 2):
        pair = shape.length // 2 - 1 - chunk * (shape.chunk // 2) - j // 2
        terms = [weight_next[mode] * state[mode] for mode in range(modes)]
        terms.append(now * ahead[pair_rows(shape, half, pair, modes), :])
        conv[rows_at(j), :] = tree_sum(terms)
        state = [
            square[mode] * state[mode] + ahead[pair_rows(shape, half, pair, mode), :]
            for mode in range(modes)
        ]
        conv[rows_at(j + 1), :] = tree_sum([weight[mode] * state[mode] for mode in range(modes)])
    return tuple(state)


def outputs(shape, half, token, pair, inputs, conv, staged):
    step = min(32, shape.chunk)

    def body(i, carry):
        at = pl.multiple_of(token + i * step, step)
        for group in range(GROUPS):
            lane = slice(group * LANES, (group + 1) * LANES)
            row = half * shape.plane + group * shape.stride + at
            rows = pl.ds(pl.multiple_of(row, GROUPS), step)
            value = conv[rows, :]
            for j in range(2):
                staged[j, half, pl.ds(at, step), lane] = (
                    inputs[2 * pair + j, half, pl.ds(at, step), lane].astype(F32) * value
                ).astype(BF16)
        return carry

    lax.fori_loop(0, shape.chunk // step, body, 0)


def token_of(shape, direction, chunk_index):
    last = shape.chunks - 1
    return pl.multiple_of(
        (chunk_index + direction * (last - 2 * chunk_index)) * shape.chunk, shape.chunk
    )


def in_copy(shape, j, half, direction, chunk, source, inputs, sem):
    rows = pl.ds(token_of(shape, direction, chunk), shape.chunk)
    return pltpu.make_async_copy(
        source.at[rows, lanes_of(half)], inputs.at[j, half, rows, :], sem.at[half * shape.chunks + chunk]
    )


def in_wait(shape, half, direction, chunk, inputs, sem):
    landed = inputs.at[:, half, pl.ds(token_of(shape, direction, chunk), shape.chunk), :]
    pltpu.make_async_copy(landed, landed, sem.at[half * shape.chunks + chunk]).wait()


def out_copy(shape, j, half, direction, chunk, staged, target, sem):
    rows = pl.ds(token_of(shape, direction, chunk), shape.chunk)
    return pltpu.make_async_copy(
        staged.at[j, half, rows, :], target.at[rows, lanes_of(half)], sem
    )


def send_out(shape, half, pair, direction, chunk, staged, targets, sem):
    for p in range(2):

        @pl.when(pair == p)
        def _():
            for j in range(2):
                out_copy(shape, j, half, direction, chunk, staged, targets[2 * p + j], sem).start()


def wait_all(array, sem):
    pltpu.make_async_copy(array, array, sem).wait()


def start_coefficients(rates_hbm, res_hbm, coef, sem):
    pltpu.make_async_copy(rates_hbm, coef.at[0], sem).start()
    pltpu.make_async_copy(res_hbm, coef.at[1], sem).start()


def first_kernel(
    shape, q, dy, v, k, rates_hbm, res_hbm,
    conv, ahead, held, inputs, sent, table, scale,
    near, coef, in_sem, coef_sem,
):
    direction = lax.axis_index("ctx")
    sources = (q, dy, v, k)
    start_coefficients(rates_hbm, res_hbm, coef, coef_sem)
    for half in range(shape.halves):
        for chunk in range(shape.chunks):
            for j in range(4):
                in_copy(shape, j, half, direction, chunk, sources[j], inputs, in_sem).start()
    wait_all(coef, coef_sem)
    scale[...] = mode_tables(coef[0], coef[1], table)
    zeros = (jnp.zeros((GROUPS, LANES), F32),) * shape.modes

    items = shape.halves * shape.chunks

    def run(way):
        in_wait(shape, 0, way, 0, inputs, in_sem)
        near_products(shape, 0, way, 0, 0, inputs, near)

        def sweep(half, _):
            factor = table_rows(table, 0, half, shape.modes, shape.groups)
            weight = table_rows(table, 1, half, shape.modes, shape.groups)

            def body(chunk, carry, weight=weight):
                item = half * shape.chunks + chunk + 1
                coming = jnp.minimum(item, items - 1)
                coming = (coming // shape.chunks, way, coming % shape.chunks)

                @pl.when(item < items)
                def _():
                    in_wait(shape, *coming, inputs, in_sem)

                return first_sweep(
                    shape, half, way, chunk, (*coming, 0), factor, weight, *carry,
                    inputs, near, conv, ahead, held,
                )

            carry = lax.fori_loop(0, shape.chunks - 1, body, (zeros, zeros, zeros[0]))
            state, dot, rest = body(shape.chunks - 1, carry, None)
            for mode in range(shape.modes):
                sent[0, mode, groups_of(half), :] = state[mode].astype(BF16)
                sent[1, mode, groups_of(half), :] = (dot[mode] + rest).astype(BF16)
            return 0

        lax.fori_loop(0, shape.halves, sweep, 0)

    for way in range(2):
        pl.when(direction == way)(functools.partial(run, way))


def early_kernel(shape, conv_in, held, inputs, table, conv, staged):
    del conv_in
    direction = lax.axis_index("ctx")
    step = 16

    def last(half, carry):
        weight = table_rows(table, 1, half, shape.modes, shape.groups)
        rows_at = rows_of(shape, half, direction, shape.chunks - 1)

        def tokens(i, carry):
            for k in range(step):
                j = i * step + k
                conv[rows_at(j), :] = tree_sum(
                    [
                        weight[mode] * held[held_rows(shape, half, j, mode), :]
                        for mode in range(shape.modes)
                    ]
                )
            return carry

        return lax.fori_loop(0, shape.chunk // step, tokens, carry)

    lax.fori_loop(0, shape.halves, last, 0)

    def body(i, carry):
        half, chunk = i // shape.chunks, i % shape.chunks
        outputs(shape, half, token_of(shape, 0, chunk), direction, inputs, conv, staged)
        return carry

    lax.fori_loop(0, shape.halves * shape.chunks, body, 0)


def early_copy(j, half, early, target, sem):
    return pltpu.make_async_copy(
        early.at[j, half], target.at[:, lanes_of(half)], sem
    )


def second_kernel(
    shape, early, ahead, inputs, sent, table, scale, received,
    out0, out1, out2, out3, residue,
    conv, staged, totals, total, out_sem, early_sem, residue_sem,
):
    owner = lax.axis_index("ctx")
    direction = 1 - owner
    targets = (out0, out1, out2, out3)
    modes = shape.modes
    for p in range(2):

        @pl.when(owner == p)
        def _():
            for j in range(2):
                for half in range(shape.halves):
                    early_copy(j, half, early, targets[2 * p + j], early_sem).start()

    def run(way):
        def sweep(half, _):
            factor = table_rows(table, 0, half, modes, shape.groups)
            weight = table_rows(table, 1, half, modes, shape.groups)
            square = [value * value for value in factor]
            weight_next = [weight[mode] * factor[mode] for mode in range(modes)]
            now = tree_sum(weight)
            state = []
            for mode in range(modes):
                mine = sent[0, mode, groups_of(half), :].astype(F32)
                theirs = received[0, mode, groups_of(half), :].astype(F32)
                mine_dot = sent[1, mode, groups_of(half), :].astype(F32)
                their_dot = received[1, mode, groups_of(half), :].astype(F32)
                totals[pl.ds(mode * GROUPS, GROUPS), :] = (
                    mine_dot + their_dot + factor[mode] * (mine * theirs)
                )
                state.append(theirs)
            for group in range(GROUPS):
                lane = lanes_of(half, group)
                total[:, lane] = totals[pl.ds(group, modes, stride=GROUPS), :] * scale[:, lane]
            lane = lanes_of(half)
            pltpu.make_async_copy(total.at[:, lane], residue.at[:, lane], residue_sem).start()

            def body(chunk, state):
                token = token_of(shape, way, chunk)
                state = second_sweep(
                    shape, half, way, chunk, square, weight, weight_next, now, state, ahead, conv
                )
                outputs(shape, half, token, way, inputs, conv, staged)
                for j in range(2):
                    out_copy(
                        shape, j, half, way, chunk, staged, targets[2 * way + j], out_sem
                    ).start()
                return state

            lax.fori_loop(0, shape.chunks, body, tuple(state))
            return 0

        lax.fori_loop(0, shape.halves, sweep, 0)

    for way in range(2):
        pl.when(direction == way)(functools.partial(run, way))

    wait_all(early, early_sem)
    wait_all(total, residue_sem)
    wait_all(staged, out_sem)


def ends_kernel(
    shape, q, dy, v, k, rates_hbm, res_hbm,
    wide, inputs, ends, table, scale,
    coef, in_sem, coef_sem,
):
    sources = (q, dy, v, k)
    start_coefficients(rates_hbm, res_hbm, coef, coef_sem)
    for half in range(shape.halves):
        for chunk in range(shape.chunks):
            for j in range(4):
                in_copy(shape, j, half, 0, chunk, sources[j], inputs, in_sem).start()
    wait_all(coef, coef_sem)
    scale[...] = mode_tables(coef[0], coef[1], table)
    zeros = (jnp.zeros((GROUPS, LANES), F32),) * shape.modes
    for half in range(shape.halves):
        factor = table_rows(table, 0, half, shape.modes, shape.groups)

        def forward(chunk, carry):
            in_wait(shape, half, 0, chunk, inputs, in_sem)
            products(shape, half, token_of(shape, 0, chunk), inputs, wide)
            state, dot = recurrence(
                shape, half, 0, chunk, factor, None, carry[0], carry[1], wide, None
            )
            return tuple(state), tuple(dot)

        def backward(chunk, state):
            state, _ = recurrence(shape, half, 1, chunk, factor, None, state, (), wide, None)
            return tuple(state)

        state, dot = lax.fori_loop(0, shape.chunks, forward, (zeros, zeros))
        back = lax.fori_loop(0, shape.chunks, backward, zeros)
        rows = groups_of(half)
        for mode in range(shape.modes):
            ends[0, mode, rows, :] = state[mode]
            ends[1, mode, rows, :] = back[mode]
            ends[2, mode, rows, :] = dot[mode]


def both_kernel(
    shape, wide, inputs, starts, table,
    out0, out1, out2, out3,
    conv, staged, out_sem,
):
    targets = (out0, out1, out2, out3)
    for direction in range(2):
        for half in range(shape.halves):
            rows = groups_of(half)
            factor = table_rows(table, 0, half, shape.modes, shape.groups)
            weight = table_rows(table, 1, half, shape.modes, shape.groups)
            state = tuple(starts[direction, mode, rows, :] for mode in range(shape.modes))

            def body(chunk, state):
                token = token_of(shape, direction, chunk)
                state, _ = recurrence(
                    shape, half, direction, chunk, factor, weight, state, (), wide, conv
                )
                outputs(shape, half, token, direction, inputs, conv, staged)
                for j in range(2):
                    out_copy(
                        shape, j, half, direction, chunk, staged, targets[2 * direction + j], out_sem
                    ).start()
                return tuple(state)

            lax.fori_loop(0, shape.chunks, body, state)
        wait_all(staged, out_sem)


HBM = pl.BlockSpec(memory_space=pltpu.HBM)
VMEM = pl.BlockSpec(memory_space=pltpu.VMEM)
LIMIT = 24 << 20


def pair(shape, arrays):
    modes, channels = shape.modes, shape.channels
    big = jax.ShapeDtypeStruct((shape.length, channels), BF16)
    copies = shape.halves * shape.chunks
    conv, ahead, held, inputs, sent, table, scale = pl.pallas_call(
        functools.partial(first_kernel, shape),
        in_specs=[HBM] * 6,
        out_specs=[VMEM] * 7,
        out_shape=[
            pltpu.VMEM((shape.rows, LANES), F32),
            pltpu.VMEM((shape.groups * shape.length // 2 * (modes + 1), LANES), F32),
            pltpu.VMEM((shape.groups * shape.chunk * modes, LANES), F32),
            pltpu.VMEM((4, shape.halves, shape.length, BLOCK), BF16),
            jax.ShapeDtypeStruct((2, modes, shape.groups, LANES), BF16),
            pltpu.VMEM((2 * modes * shape.groups, LANES), F32),
            pltpu.VMEM((modes, channels), F32),
        ],
        scratch_shapes=[
            pltpu.VMEM((2, (shape.chunk + PAD) * GROUPS, LANES), F32),
            pltpu.VMEM((2, modes, channels), F32),
            pltpu.SemaphoreType.DMA((copies,)),
            pltpu.SemaphoreType.DMA,
        ],
        compiler_params=pltpu.CompilerParams(vmem_limit_bytes=LIMIT),
        name="first",
    )(*arrays)
    received = lax.ppermute(sent, "ctx", [(0, 1), (1, 0)])
    _, early = pl.pallas_call(
        functools.partial(early_kernel, shape),
        in_specs=[VMEM] * 4,
        out_specs=[VMEM] * 2,
        out_shape=[
            pltpu.VMEM((shape.rows, LANES), F32),
            pltpu.VMEM((2, shape.halves, shape.length, BLOCK), BF16),
        ],
        input_output_aliases={0: 0},
        compiler_params=pltpu.CompilerParams(vmem_limit_bytes=LIMIT),
        name="early",
    )(conv, held, inputs, table)
    *outs, residue = pl.pallas_call(
        functools.partial(second_kernel, shape),
        in_specs=[VMEM] * 7,
        out_specs=[HBM] * 5,
        out_shape=[big] * 4 + [jax.ShapeDtypeStruct((modes, channels), F32)],
        scratch_shapes=[
            pltpu.VMEM((shape.rows, LANES), F32),
            pltpu.VMEM((2, shape.halves, shape.length, BLOCK), BF16),
            pltpu.VMEM((modes * GROUPS, LANES), F32),
            pltpu.VMEM((modes, channels), F32),
            pltpu.SemaphoreType.DMA,
            pltpu.SemaphoreType.DMA,
            pltpu.SemaphoreType.DMA,
        ],
        compiler_params=pltpu.CompilerParams(vmem_limit_bytes=LIMIT),
        name="second",
    )(early, ahead, inputs, sent, table, scale, received)
    return outs, residue


def many(shape, arrays, rates, owners):
    modes, channels = shape.modes, shape.channels
    big = jax.ShapeDtypeStruct((shape.length, channels), BF16)
    copies = shape.halves * shape.chunks
    wide, inputs, ends, table, scale = pl.pallas_call(
        functools.partial(ends_kernel, shape),
        in_specs=[HBM] * 6,
        out_specs=[VMEM] * 5,
        out_shape=[
            pltpu.VMEM((2, shape.rows, LANES), F32),
            pltpu.VMEM((4, shape.halves, shape.length, BLOCK), BF16),
            jax.ShapeDtypeStruct((3, modes, shape.groups, LANES), F32),
            pltpu.VMEM((2 * modes * shape.groups, LANES), F32),
            jax.ShapeDtypeStruct((modes, channels), F32),
        ],
        scratch_shapes=[
            pltpu.VMEM((2, modes, channels), F32),
            pltpu.SemaphoreType.DMA((copies,)),
            pltpu.SemaphoreType.DMA,
        ],
        compiler_params=pltpu.CompilerParams(vmem_limit_bytes=LIMIT),
        name="ends",
    )(*arrays)
    rates = rates.reshape(modes, shape.groups, LANES)
    here = lax.axis_index("ctx")
    parts = lax.all_gather(ends[:2].astype(BF16), "ctx", axis=0).astype(F32)
    owner = jnp.arange(owners, dtype=jnp.int32)
    gaps = jnp.stack([here - 1 - owner, owner - 1 - here], axis=1).astype(F32)[:, :, None, None, None]
    decay = jnp.exp(-rates * shape.length * jnp.maximum(gaps, 0.0))
    starts = jnp.sum(jnp.where(gaps >= 0, decay, 0.0) * parts, axis=0)
    dots = ends[2] + jnp.exp(-rates) * ends[1] * starts[0]
    total = jnp.sum(lax.all_gather(dots.astype(BF16), "ctx", axis=0).astype(F32), axis=0)
    residue = total.reshape(modes, channels) * scale
    outs = pl.pallas_call(
        functools.partial(both_kernel, shape),
        in_specs=[VMEM] * 4,
        out_specs=[HBM] * 4,
        out_shape=[big] * 4,
        scratch_shapes=[
            pltpu.VMEM((shape.rows, LANES), F32),
            pltpu.VMEM((2, shape.halves, shape.length, BLOCK), BF16),
            pltpu.SemaphoreType.DMA,
        ],
        compiler_params=pltpu.CompilerParams(vmem_limit_bytes=LIMIT),
        name="both",
    )(wide, inputs, starts, table)
    return outs, residue


def body(owners, query_branch, key_branch, value_branch, output_grad, residues, decay_rates):
    length, channels = query_branch.shape
    rates = decay_rates.T
    shape = Shape(length, channels, rates.shape[0])
    hbm = functools.partial(pltpu.with_memory_space_constraint, memory_space=pltpu.HBM)
    arrays = [
        hbm(array)
        for array in (query_branch, output_grad, value_branch, key_branch, rates, residues.T)
    ]
    outs, residue = pair(shape, arrays) if owners == 2 else many(shape, arrays, rates, owners)
    mixed_out, query_grad, key_grad, value_grad = outs
    return (mixed_out, query_grad, key_grad, value_grad, residue.T)


def solution(mesh):
    tokens = P(("dp", "ctx"), "tp")
    return jax.shard_map(
        functools.partial(body, mesh.shape["ctx"]),
        mesh=mesh,
        in_specs=(tokens,) * 4 + (P("tp", None),) * 2,
        out_specs=(tokens,) * 4 + (P(("dp", "tp"), None),),
        check_vma=False,
    )
```

```python
import functools

import jax
import jax.numpy as jnp
from jax import lax
from jax.experimental import pallas as pl
from jax.experimental.pallas import tpu as pltpu
from jax.sharding import PartitionSpec as P

F32 = jnp.float32
BF16 = jnp.bfloat16
LANES = 128
GROUPS = 8
BLOCK = GROUPS * LANES
PAD = 8
UNROLL = 64


def one_minus_exp_2(rate, factor):
    square = rate * rate
    sinh = rate * (1.0 + square * (1 / 6 + square * (1 / 120 + square * (1 / 5040))))
    return 2.0 * factor * sinh


def mode_tables(rates, residues, table):
    modes, channels = rates.shape
    factor = jnp.exp(-rates)
    scale = jnp.sqrt(one_minus_exp_2(rates, factor) / modes)
    weight = residues * scale
    groups = channels // LANES
    for group in range(groups):
        lanes = slice(group * LANES, (group + 1) * LANES)
        table[pl.ds(group * modes, modes), :] = factor[:, lanes]
        table[pl.ds((groups + group) * modes, modes), :] = weight[:, lanes]
    return scale


def table_rows(table, which, half, modes, groups):
    start = (which * groups + half * GROUPS) * modes
    return [table[pl.ds(start + mode, GROUPS, stride=modes), :] for mode in range(modes)]


def tree_sum(terms):
    while len(terms) > 1:
        terms = [
            terms[i] + terms[i + 1] if i + 1 < len(terms) else terms[i]
            for i in range(0, len(terms), 2)
        ]
    return terms[0]


class Shape:
    def __init__(self, length, channels, modes):
        self.length = length
        self.channels = channels
        self.modes = modes
        self.halves = channels // BLOCK
        self.groups = channels // LANES
        self.chunk = min(64, length)
        self.chunks = length // self.chunk
        self.stride = length + PAD
        self.plane = GROUPS * self.stride
        self.rows = self.halves * self.plane


def lanes_of(half, group=None):
    if group is None:
        return pl.ds(pl.multiple_of(half * BLOCK, BLOCK), BLOCK)
    return pl.ds(pl.multiple_of(half * BLOCK + group * LANES, LANES), LANES)


def groups_of(half):
    return pl.ds(pl.multiple_of(half * GROUPS, GROUPS), GROUPS)


def products(shape, half, token, inputs, wide):
    step = min(32, shape.chunk)

    def body(i, carry):
        at = pl.multiple_of(token + i * step, step)
        for group in range(GROUPS):
            lane = slice(group * LANES, (group + 1) * LANES)
            row = half * shape.plane + group * shape.stride + at
            rows = pl.ds(pl.multiple_of(row, GROUPS), step)
            q, dy, v, k = [inputs[j, half, pl.ds(at, step), lane] for j in range(4)]
            wide[0, rows, :] = (k * v).astype(F32)
            wide[1, rows, :] = (dy * q).astype(F32)
        return carry

    lax.fori_loop(0, shape.chunk // step, body, 0)


def recurrence(shape, half, direction, chunk_index, factor, weight, state, dot, wide, conv):
    sign = 1 - 2 * direction
    begin = direction * (shape.length - 1) + sign * chunk_index * shape.chunk
    begin = half * shape.plane + begin
    steps = [sign * j for j in range(UNROLL)]
    stride = sign * UNROLL
    modes = shape.modes

    def body(i, carry):
        state, dot = list(carry[0]), list(carry[1])
        for j in range(UNROLL):
            rows = pl.ds(begin + i * stride + steps[j], GROUPS, stride=shape.stride)
            source = wide[direction, rows, :]
            other = wide[1 - direction, rows, :] if dot else None
            terms = []
            for mode in range(modes):
                state[mode] = factor[mode] * state[mode] + source
                if weight is not None:
                    terms.append(weight[mode] * state[mode])
                if dot:
                    dot[mode] = dot[mode] + other * state[mode]
            if weight is not None:
                conv[rows, :] = tree_sum(terms)
        return tuple(state), tuple(dot)

    state, dot = lax.fori_loop(0, shape.chunk // UNROLL, body, (tuple(state), tuple(dot)))
    return list(state), list(dot)


def rows_of(shape, half, direction, chunk):
    sign = 1 - 2 * direction
    begin = half * shape.plane + direction * (shape.length - 1) + sign * chunk * shape.chunk
    return lambda j: pl.ds(begin + sign * j, GROUPS, stride=shape.stride)


def pair_rows(shape, half, pair, slot):
    row = ((half * (shape.length // 2) + pair) * (shape.modes + 1) + slot) * GROUPS
    return pl.ds(pl.multiple_of(row, GROUPS), GROUPS)


def held_rows(shape, half, j, mode):
    row = ((half * shape.chunk + j) * shape.modes + mode) * GROUPS
    return pl.ds(pl.multiple_of(row, GROUPS), GROUPS)


def near_products(shape, half, direction, chunk, index, inputs, near):
    start = shape.chunk - 8 - 8 * index if direction else 8 * index
    at = pl.multiple_of(token_of(shape, direction, chunk) + start, 8)
    first, second = 2 * (1 - direction), 2 * direction
    for group in range(GROUPS):
        lane = slice(group * LANES, (group + 1) * LANES)
        rows = pl.ds(group * (shape.chunk + PAD) + start, 8)
        a0, a1, b0, b1 = [
            inputs[plane + j, half, pl.ds(at, 8), lane] for plane in (first, second) for j in range(2)
        ]
        near[0, rows, :] = (a0 * a1).astype(F32)
        near[1, rows, :] = (b0 * b1).astype(F32)


def first_sweep(
    shape, half, direction, chunk, coming, factor, weight, state, dot, rest,
    inputs, near, conv, ahead, held,
):
    rows_at = rows_of(shape, half, direction, chunk)
    modes = shape.modes
    state, dot = list(state), list(dot)

    def emit(j, state):
        if weight is not None:
            conv[rows_at(j), :] = tree_sum([weight[mode] * state[mode] for mode in range(modes)])
            return
        for mode in range(modes):
            held[held_rows(shape, half, j, mode), :] = state[mode]

    def near_row(j):
        token = shape.chunk - 1 - j if direction else j
        return pl.ds(token, GROUPS, stride=shape.chunk + PAD)

    for j in range(0, shape.chunk, 2):
        if j % 8 == 0:
            index = j // 8 + 1
            if index < shape.chunk // 8:
                near_products(shape, half, direction, chunk, index, inputs, near)
        pair = chunk * (shape.chunk // 2) + j // 2
        source0, source1 = near[0, near_row(j), :], near[0, near_row(j + 1), :]
        other0, other1 = near[1, near_row(j), :], near[1, near_row(j + 1), :]
        state = [factor[mode] * state[mode] + source0 for mode in range(modes)]
        emit(j, state)
        for mode in range(modes):
            both = other0 + factor[mode] * other1
            ahead[pair_rows(shape, half, pair, mode), :] = both
            dot[mode] = dot[mode] + state[mode] * both
        rest = rest + source1 * other1
        ahead[pair_rows(shape, half, pair, modes), :] = other1
        state = [factor[mode] * state[mode] + source1 for mode in range(modes)]
        emit(j + 1, state)
    near_products(shape, *coming, inputs, near)
    return tuple(state), tuple(dot), rest


def second_sweep(shape, half, direction, chunk, square, weight, weight_next, now, state, ahead, conv):
    rows_at = rows_of(shape, half, direction, chunk)
    modes = shape.modes
    state = list(state)
    for j in range(0, shape.chunk, 2):
        pair = shape.length // 2 - 1 - chunk * (shape.chunk // 2) - j // 2
        terms = [weight_next[mode] * state[mode] for mode in range(modes)]
        terms.append(now * ahead[pair_rows(shape, half, pair, modes), :])
        conv[rows_at(j), :] = tree_sum(terms)
        state = [
            square[mode] * state[mode] + ahead[pair_rows(shape, half, pair, mode), :]
            for mode in range(modes)
        ]
        conv[rows_at(j + 1), :] = tree_sum([weight[mode] * state[mode] for mode in range(modes)])
    return tuple(state)


def outputs(shape, half, token, pair, inputs, conv, staged):
    step = min(32, shape.chunk)

    def body(i, carry):
        at = pl.multiple_of(token + i * step, step)
        for group in range(GROUPS):
            lane = slice(group * LANES, (group + 1) * LANES)
            row = half * shape.plane + group * shape.stride + at
            rows = pl.ds(pl.multiple_of(row, GROUPS), step)
            value = conv[rows, :]
            for j in range(2):
                staged[j, half, pl.ds(at, step), lane] = (
                    inputs[2 * pair + j, half, pl.ds(at, step), lane].astype(F32) * value
                ).astype(BF16)
        return carry

    lax.fori_loop(0, shape.chunk // step, body, 0)


def token_of(shape, direction, chunk_index):
    last = shape.chunks - 1
    return pl.multiple_of(
        (chunk_index + direction * (last - 2 * chunk_index)) * shape.chunk, shape.chunk
    )


def in_copy(shape, j, half, direction, chunk, source, inputs, sem):
    rows = pl.ds(token_of(shape, direction, chunk), shape.chunk)
    return pltpu.make_async_copy(
        source.at[rows, lanes_of(half)], inputs.at[j, half, rows, :], sem.at[half * shape.chunks + chunk]
    )


def in_wait(shape, half, direction, chunk, inputs, sem):
    landed = inputs.at[:, half, pl.ds(token_of(shape, direction, chunk), shape.chunk), :]
    pltpu.make_async_copy(landed, landed, sem.at[half * shape.chunks + chunk]).wait()


def split_rows(shape, direction):
    half, chunk = 1 // shape.chunks, 1 % shape.chunks
    token = token_of(shape, direction, chunk)
    head = pl.multiple_of(token + direction * (shape.chunk - 8), 8)
    rest = pl.multiple_of(token + (1 - direction) * 8, 8)
    return half, pl.ds(head, 8), pl.ds(rest, shape.chunk - 8)


def split_wait(shape, direction, which, inputs, sem):
    half, *parts = split_rows(shape, direction)
    landed = inputs.at[:, half, parts[which], :]
    index = shape.halves * shape.chunks if which else 1
    pltpu.make_async_copy(landed, landed, sem.at[index]).wait()


def out_copy(shape, j, half, direction, chunk, staged, target, sem):
    rows = pl.ds(token_of(shape, direction, chunk), shape.chunk)
    return pltpu.make_async_copy(
        staged.at[j, half, rows, :], target.at[rows, lanes_of(half)], sem
    )


def send_out(shape, half, pair, direction, chunk, staged, targets, sem):
    for p in range(2):

        @pl.when(pair == p)
        def _():
            for j in range(2):
                out_copy(shape, j, half, direction, chunk, staged, targets[2 * p + j], sem).start()


def wait_all(array, sem):
    pltpu.make_async_copy(array, array, sem).wait()


def start_coefficients(rates_hbm, res_hbm, coef, sem):
    pltpu.make_async_copy(rates_hbm, coef.at[0], sem).start()
    pltpu.make_async_copy(res_hbm, coef.at[1], sem).start()


def first_kernel(
    shape, q, dy, v, k, rates_hbm, res_hbm,
    conv, ahead, held, inputs, sent, table, scale,
    near, coef, in_sem, coef_sem,
):
    direction = lax.axis_index("ctx")
    sources = (q, dy, v, k)
    start_coefficients(rates_hbm, res_hbm, coef, coef_sem)
    items = shape.halves * shape.chunks
    for item in range(items):
        if item == 1:
            half, *parts = split_rows(shape, direction)
            for tokens, index in zip(parts, (1, items)):
                for j in range(4):
                    pltpu.make_async_copy(
                        sources[j].at[tokens, lanes_of(half)],
                        inputs.at[j, half, tokens, :],
                        in_sem.at[index],
                    ).start()
            continue
        half, chunk = item // shape.chunks, item % shape.chunks
        for j in range(4):
            in_copy(shape, j, half, direction, chunk, sources[j], inputs, in_sem).start()
    wait_all(coef, coef_sem)
    scale[...] = mode_tables(coef[0], coef[1], table)
    zeros = (jnp.zeros((GROUPS, LANES), F32),) * shape.modes

    def run(way):
        in_wait(shape, 0, way, 0, inputs, in_sem)
        near_products(shape, 0, way, 0, 0, inputs, near)

        def sweep(half, _):
            factor = table_rows(table, 0, half, shape.modes, shape.groups)
            weight = table_rows(table, 1, half, shape.modes, shape.groups)

            def body(chunk, carry, weight=weight):
                item = half * shape.chunks + chunk + 1
                coming = jnp.minimum(item, items - 1)
                coming = (coming // shape.chunks, way, coming % shape.chunks)

                @pl.when((item < items) & (item != 1))
                def _():
                    in_wait(shape, *coming, inputs, in_sem)

                for which in range(2):
                    pl.when(item == 1 + which)(
                        functools.partial(split_wait, shape, way, which, inputs, in_sem)
                    )

                return first_sweep(
                    shape, half, way, chunk, (*coming, 0), factor, weight, *carry,
                    inputs, near, conv, ahead, held,
                )

            carry = lax.fori_loop(0, shape.chunks - 1, body, (zeros, zeros, zeros[0]))
            state, dot, rest = body(shape.chunks - 1, carry, None)
            for mode in range(shape.modes):
                sent[0, mode, groups_of(half), :] = state[mode].astype(BF16)
                sent[1, mode, groups_of(half), :] = (dot[mode] + rest).astype(BF16)
            return 0

        lax.fori_loop(0, shape.halves, sweep, 0)

    for way in range(2):
        pl.when(direction == way)(functools.partial(run, way))


def early_kernel(shape, conv_in, held, inputs, table, conv, staged):
    del conv_in
    direction = lax.axis_index("ctx")
    step = 16

    def last(half, carry):
        weight = table_rows(table, 1, half, shape.modes, shape.groups)
        rows_at = rows_of(shape, half, direction, shape.chunks - 1)

        def tokens(i, carry):
            for k in range(step):
                j = i * step + k
                conv[rows_at(j), :] = tree_sum(
                    [
                        weight[mode] * held[held_rows(shape, half, j, mode), :]
                        for mode in range(shape.modes)
                    ]
                )
            return carry

        return lax.fori_loop(0, shape.chunk // step, tokens, carry)

    lax.fori_loop(0, shape.halves, last, 0)

    def body(i, carry):
        half, chunk = i // shape.chunks, i % shape.chunks
        outputs(shape, half, token_of(shape, 0, chunk), direction, inputs, conv, staged)
        return carry

    lax.fori_loop(0, shape.halves * shape.chunks, body, 0)


def early_copy(j, half, early, target, sem):
    return pltpu.make_async_copy(
        early.at[j, half], target.at[:, lanes_of(half)], sem
    )


def second_kernel(
    shape, early, ahead, inputs, sent, table, scale, received,
    out0, out1, out2, out3, residue,
    conv, staged, totals, total, out_sem, early_sem, residue_sem,
):
    owner = lax.axis_index("ctx")
    direction = 1 - owner
    targets = (out0, out1, out2, out3)
    modes = shape.modes
    for p in range(2):

        @pl.when(owner == p)
        def _():
            for j in range(2):
                for half in range(shape.halves):
                    early_copy(j, half, early, targets[2 * p + j], early_sem).start()

    def run(way):
        def sweep(half, _):
            factor = table_rows(table, 0, half, modes, shape.groups)
            weight = table_rows(table, 1, half, modes, shape.groups)
            square = [value * value for value in factor]
            weight_next = [weight[mode] * factor[mode] for mode in range(modes)]
            now = tree_sum(weight)
            state = []
            for mode in range(modes):
                mine = sent[0, mode, groups_of(half), :].astype(F32)
                theirs = received[0, mode, groups_of(half), :].astype(F32)
                mine_dot = sent[1, mode, groups_of(half), :].astype(F32)
                their_dot = received[1, mode, groups_of(half), :].astype(F32)
                totals[pl.ds(mode * GROUPS, GROUPS), :] = (
                    mine_dot + their_dot + factor[mode] * (mine * theirs)
                )
                state.append(theirs)
            for group in range(GROUPS):
                lane = lanes_of(half, group)
                total[:, lane] = totals[pl.ds(group, modes, stride=GROUPS), :] * scale[:, lane]
            lane = lanes_of(half)
            pltpu.make_async_copy(total.at[:, lane], residue.at[:, lane], residue_sem).start()

            def body(chunk, state):
                token = token_of(shape, way, chunk)
                state = second_sweep(
                    shape, half, way, chunk, square, weight, weight_next, now, state, ahead, conv
                )
                outputs(shape, half, token, way, inputs, conv, staged)
                for j in range(2):
                    out_copy(
                        shape, j, half, way, chunk, staged, targets[2 * way + j], out_sem
                    ).start()
                return state

            lax.fori_loop(0, shape.chunks, body, tuple(state))
            return 0

        lax.fori_loop(0, shape.halves, sweep, 0)

    for way in range(2):
        pl.when(direction == way)(functools.partial(run, way))

    wait_all(early, early_sem)
    wait_all(total, residue_sem)
    wait_all(staged, out_sem)


def ends_kernel(
    shape, q, dy, v, k, rates_hbm, res_hbm,
    wide, inputs, ends, table, scale,
    coef, in_sem, coef_sem,
):
    sources = (q, dy, v, k)
    start_coefficients(rates_hbm, res_hbm, coef, coef_sem)
    for half in range(shape.halves):
        for chunk in range(shape.chunks):
            for j in range(4):
                in_copy(shape, j, half, 0, chunk, sources[j], inputs, in_sem).start()
    wait_all(coef, coef_sem)
    scale[...] = mode_tables(coef[0], coef[1], table)
    zeros = (jnp.zeros((GROUPS, LANES), F32),) * shape.modes
    for half in range(shape.halves):
        factor = table_rows(table, 0, half, shape.modes, shape.groups)

        def forward(chunk, carry):
            in_wait(shape, half, 0, chunk, inputs, in_sem)
            products(shape, half, token_of(shape, 0, chunk), inputs, wide)
            state, dot = recurrence(
                shape, half, 0, chunk, factor, None, carry[0], carry[1], wide, None
            )
            return tuple(state), tuple(dot)

        def backward(chunk, state):
            state, _ = recurrence(shape, half, 1, chunk, factor, None, state, (), wide, None)
            return tuple(state)

        state, dot = lax.fori_loop(0, shape.chunks, forward, (zeros, zeros))
        back = lax.fori_loop(0, shape.chunks, backward, zeros)
        rows = groups_of(half)
        for mode in range(shape.modes):
            ends[0, mode, rows, :] = state[mode]
            ends[1, mode, rows, :] = back[mode]
            ends[2, mode, rows, :] = dot[mode]


def both_kernel(
    shape, wide, inputs, starts, table,
    out0, out1, out2, out3,
    conv, staged, out_sem,
):
    targets = (out0, out1, out2, out3)
    for direction in range(2):
        for half in range(shape.halves):
            rows = groups_of(half)
            factor = table_rows(table, 0, half, shape.modes, shape.groups)
            weight = table_rows(table, 1, half, shape.modes, shape.groups)
            state = tuple(starts[direction, mode, rows, :] for mode in range(shape.modes))

            def body(chunk, state):
                token = token_of(shape, direction, chunk)
                state, _ = recurrence(
                    shape, half, direction, chunk, factor, weight, state, (), wide, conv
                )
                outputs(shape, half, token, direction, inputs, conv, staged)
                for j in range(2):
                    out_copy(
                        shape, j, half, direction, chunk, staged, targets[2 * direction + j], out_sem
                    ).start()
                return tuple(state)

            lax.fori_loop(0, shape.chunks, body, state)
        wait_all(staged, out_sem)


HBM = pl.BlockSpec(memory_space=pltpu.HBM)
VMEM = pl.BlockSpec(memory_space=pltpu.VMEM)
LIMIT = 24 << 20


def pair(shape, arrays):
    modes, channels = shape.modes, shape.channels
    big = jax.ShapeDtypeStruct((shape.length, channels), BF16)
    copies = shape.halves * shape.chunks
    conv, ahead, held, inputs, sent, table, scale = pl.pallas_call(
        functools.partial(first_kernel, shape),
        in_specs=[HBM] * 6,
        out_specs=[VMEM] * 7,
        out_shape=[
            pltpu.VMEM((shape.rows, LANES), F32),
            pltpu.VMEM((shape.groups * shape.length // 2 * (modes + 1), LANES), F32),
            pltpu.VMEM((shape.groups * shape.chunk * modes, LANES), F32),
            pltpu.VMEM((4, shape.halves, shape.length, BLOCK), BF16),
            jax.ShapeDtypeStruct((2, modes, shape.groups, LANES), BF16),
            pltpu.VMEM((2 * modes * shape.groups, LANES), F32),
            pltpu.VMEM((modes, channels), F32),
        ],
        scratch_shapes=[
            pltpu.VMEM((2, (shape.chunk + PAD) * GROUPS, LANES), F32),
            pltpu.VMEM((2, modes, channels), F32),
            pltpu.SemaphoreType.DMA((copies + 1,)),
            pltpu.SemaphoreType.DMA,
        ],
        compiler_params=pltpu.CompilerParams(vmem_limit_bytes=LIMIT),
        name="first",
    )(*arrays)
    received = lax.ppermute(sent, "ctx", [(0, 1), (1, 0)])
    _, early = pl.pallas_call(
        functools.partial(early_kernel, shape),
        in_specs=[VMEM] * 4,
        out_specs=[VMEM] * 2,
        out_shape=[
            pltpu.VMEM((shape.rows, LANES), F32),
            pltpu.VMEM((2, shape.halves, shape.length, BLOCK), BF16),
        ],
        input_output_aliases={0: 0},
        compiler_params=pltpu.CompilerParams(vmem_limit_bytes=LIMIT),
        name="early",
    )(conv, held, inputs, table)
    *outs, residue = pl.pallas_call(
        functools.partial(second_kernel, shape),
        in_specs=[VMEM] * 7,
        out_specs=[HBM] * 5,
        out_shape=[big] * 4 + [jax.ShapeDtypeStruct((modes, channels), F32)],
        scratch_shapes=[
            pltpu.VMEM((shape.rows, LANES), F32),
            pltpu.VMEM((2, shape.halves, shape.length, BLOCK), BF16),
            pltpu.VMEM((modes * GROUPS, LANES), F32),
            pltpu.VMEM((modes, channels), F32),
            pltpu.SemaphoreType.DMA,
            pltpu.SemaphoreType.DMA,
            pltpu.SemaphoreType.DMA,
        ],
        compiler_params=pltpu.CompilerParams(vmem_limit_bytes=LIMIT),
        name="second",
    )(early, ahead, inputs, sent, table, scale, received)
    return outs, residue


def many(shape, arrays, rates, owners):
    modes, channels = shape.modes, shape.channels
    big = jax.ShapeDtypeStruct((shape.length, channels), BF16)
    copies = shape.halves * shape.chunks
    wide, inputs, ends, table, scale = pl.pallas_call(
        functools.partial(ends_kernel, shape),
        in_specs=[HBM] * 6,
        out_specs=[VMEM] * 5,
        out_shape=[
            pltpu.VMEM((2, shape.rows, LANES), F32),
            pltpu.VMEM((4, shape.halves, shape.length, BLOCK), BF16),
            jax.ShapeDtypeStruct((3, modes, shape.groups, LANES), F32),
            pltpu.VMEM((2 * modes * shape.groups, LANES), F32),
            jax.ShapeDtypeStruct((modes, channels), F32),
        ],
        scratch_shapes=[
            pltpu.VMEM((2, modes, channels), F32),
            pltpu.SemaphoreType.DMA((copies,)),
            pltpu.SemaphoreType.DMA,
        ],
        compiler_params=pltpu.CompilerParams(vmem_limit_bytes=LIMIT),
        name="ends",
    )(*arrays)
    rates = rates.reshape(modes, shape.groups, LANES)
    here = lax.axis_index("ctx")
    parts = lax.all_gather(ends[:2].astype(BF16), "ctx", axis=0).astype(F32)
    owner = jnp.arange(owners, dtype=jnp.int32)
    gaps = jnp.stack([here - 1 - owner, owner - 1 - here], axis=1).astype(F32)[:, :, None, None, None]
    decay = jnp.exp(-rates * shape.length * jnp.maximum(gaps, 0.0))
    starts = jnp.sum(jnp.where(gaps >= 0, decay, 0.0) * parts, axis=0)
    dots = ends[2] + jnp.exp(-rates) * ends[1] * starts[0]
    total = jnp.sum(lax.all_gather(dots.astype(BF16), "ctx", axis=0).astype(F32), axis=0)
    residue = total.reshape(modes, channels) * scale
    outs = pl.pallas_call(
        functools.partial(both_kernel, shape),
        in_specs=[VMEM] * 4,
        out_specs=[HBM] * 4,
        out_shape=[big] * 4,
        scratch_shapes=[
            pltpu.VMEM((shape.rows, LANES), F32),
            pltpu.VMEM((2, shape.halves, shape.length, BLOCK), BF16),
            pltpu.SemaphoreType.DMA,
        ],
        compiler_params=pltpu.CompilerParams(vmem_limit_bytes=LIMIT),
        name="both",
    )(wide, inputs, starts, table)
    return outs, residue


def body(owners, query_branch, key_branch, value_branch, output_grad, residues, decay_rates):
    length, channels = query_branch.shape
    rates = decay_rates.T
    shape = Shape(length, channels, rates.shape[0])
    hbm = functools.partial(pltpu.with_memory_space_constraint, memory_space=pltpu.HBM)
    arrays = [
        hbm(array)
        for array in (query_branch, output_grad, value_branch, key_branch, rates, residues.T)
    ]
    outs, residue = pair(shape, arrays) if owners == 2 else many(shape, arrays, rates, owners)
    mixed_out, query_grad, key_grad, value_grad = outs
    return (mixed_out, query_grad, key_grad, value_grad, residue.T)


def solution(mesh):
    tokens = P(("dp", "ctx"), "tp")
    return jax.shard_map(
        functools.partial(body, mesh.shape["ctx"]),
        mesh=mesh,
        in_specs=(tokens,) * 4 + (P("tp", None),) * 2,
        out_specs=(tokens,) * 4 + (P(("dp", "tp"), None),),
        check_vma=False,
    )
```

```python
import functools

import jax
import jax.numpy as jnp
from jax import lax
from jax.experimental import pallas as pl
from jax.experimental.pallas import tpu as pltpu
from jax.sharding import PartitionSpec as P

F32 = jnp.float32
BF16 = jnp.bfloat16
LANES = 128
GROUPS = 8
BLOCK = GROUPS * LANES
PAD = 8
UNROLL = 64


def one_minus_exp_2(rate, factor):
    square = rate * rate
    sinh = rate * (1.0 + square * (1 / 6 + square * (1 / 120 + square * (1 / 5040))))
    return 2.0 * factor * sinh


def mode_tables(rates, residues, table):
    modes, channels = rates.shape
    factor = jnp.exp(-rates)
    scale = jnp.sqrt(one_minus_exp_2(rates, factor) / modes)
    weight = residues * scale
    groups = channels // LANES
    for group in range(groups):
        lanes = slice(group * LANES, (group + 1) * LANES)
        table[pl.ds(group * modes, modes), :] = factor[:, lanes]
        table[pl.ds((groups + group) * modes, modes), :] = weight[:, lanes]
    return scale


def table_rows(table, which, half, modes, groups):
    start = (which * groups + half * GROUPS) * modes
    return [table[pl.ds(start + mode, GROUPS, stride=modes), :] for mode in range(modes)]


def tree_sum(terms):
    while len(terms) > 1:
        terms = [
            terms[i] + terms[i + 1] if i + 1 < len(terms) else terms[i]
            for i in range(0, len(terms), 2)
        ]
    return terms[0]


class Shape:
    def __init__(self, length, channels, modes):
        self.length = length
        self.channels = channels
        self.modes = modes
        self.halves = channels // BLOCK
        self.groups = channels // LANES
        self.chunk = min(64, length)
        self.chunks = length // self.chunk
        self.stride = length + PAD
        self.plane = GROUPS * self.stride
        self.rows = self.halves * self.plane


def lanes_of(half, group=None):
    if group is None:
        return pl.ds(pl.multiple_of(half * BLOCK, BLOCK), BLOCK)
    return pl.ds(pl.multiple_of(half * BLOCK + group * LANES, LANES), LANES)


def groups_of(half):
    return pl.ds(pl.multiple_of(half * GROUPS, GROUPS), GROUPS)


def products(shape, half, token, inputs, wide):
    step = min(32, shape.chunk)

    def body(i, carry):
        at = pl.multiple_of(token + i * step, step)
        for group in range(GROUPS):
            lane = slice(group * LANES, (group + 1) * LANES)
            row = half * shape.plane + group * shape.stride + at
            rows = pl.ds(pl.multiple_of(row, GROUPS), step)
            q, dy, v, k = [inputs[j, half, pl.ds(at, step), lane] for j in range(4)]
            wide[0, rows, :] = (k * v).astype(F32)
            wide[1, rows, :] = (dy * q).astype(F32)
        return carry

    lax.fori_loop(0, shape.chunk // step, body, 0)


def recurrence(shape, half, direction, chunk_index, factor, weight, state, dot, wide, conv):
    sign = 1 - 2 * direction
    begin = direction * (shape.length - 1) + sign * chunk_index * shape.chunk
    begin = half * shape.plane + begin
    steps = [sign * j for j in range(UNROLL)]
    stride = sign * UNROLL
    modes = shape.modes

    def body(i, carry):
        state, dot = list(carry[0]), list(carry[1])
        for j in range(UNROLL):
            rows = pl.ds(begin + i * stride + steps[j], GROUPS, stride=shape.stride)
            source = wide[direction, rows, :]
            other = wide[1 - direction, rows, :] if dot else None
            terms = []
            for mode in range(modes):
                state[mode] = factor[mode] * state[mode] + source
                if weight is not None:
                    terms.append(weight[mode] * state[mode])
                if dot:
                    dot[mode] = dot[mode] + other * state[mode]
            if weight is not None:
                conv[rows, :] = tree_sum(terms)
        return tuple(state), tuple(dot)

    state, dot = lax.fori_loop(0, shape.chunk // UNROLL, body, (tuple(state), tuple(dot)))
    return list(state), list(dot)


def rows_of(shape, half, direction, chunk):
    sign = 1 - 2 * direction
    begin = half * shape.plane + direction * (shape.length - 1) + sign * chunk * shape.chunk
    return lambda j: pl.ds(begin + sign * j, GROUPS, stride=shape.stride)


def pair_rows(shape, half, pair, slot):
    row = ((half * (shape.length // 2) + pair) * (shape.modes + 1) + slot) * GROUPS
    return pl.ds(pl.multiple_of(row, GROUPS), GROUPS)


def held_rows(shape, half, j, mode):
    row = ((half * shape.chunk + j) * shape.modes + mode) * GROUPS
    return pl.ds(pl.multiple_of(row, GROUPS), GROUPS)


def near_products(shape, half, direction, chunk, index, inputs, near):
    start = shape.chunk - 8 - 8 * index if direction else 8 * index
    at = pl.multiple_of(token_of(shape, direction, chunk) + start, 8)
    first, second = 2 * (1 - direction), 2 * direction
    for group in range(GROUPS):
        lane = slice(group * LANES, (group + 1) * LANES)
        rows = pl.ds(group * (shape.chunk + PAD) + start, 8)
        a0, a1, b0, b1 = [
            inputs[plane + j, half, pl.ds(at, 8), lane] for plane in (first, second) for j in range(2)
        ]
        near[0, rows, :] = (a0 * a1).astype(F32)
        near[1, rows, :] = (b0 * b1).astype(F32)


def first_sweep(
    shape, half, direction, chunk, coming, factor, weight, state, dot, rest,
    inputs, near, conv, ahead, held,
):
    rows_at = rows_of(shape, half, direction, chunk)
    modes = shape.modes
    state, dot = list(state), list(dot)

    def emit(j, state):
        if weight is not None:
            conv[rows_at(j), :] = tree_sum([weight[mode] * state[mode] for mode in range(modes)])
            return
        for mode in range(modes):
            held[held_rows(shape, half, j, mode), :] = state[mode]

    def near_row(j):
        token = shape.chunk - 1 - j if direction else j
        return pl.ds(token, GROUPS, stride=shape.chunk + PAD)

    for j in range(0, shape.chunk, 2):
        if j % 8 == 0:
            index = j // 8 + 1
            if index < shape.chunk // 8:
                near_products(shape, half, direction, chunk, index, inputs, near)
        pair = chunk * (shape.chunk // 2) + j // 2
        source0, source1 = near[0, near_row(j), :], near[0, near_row(j + 1), :]
        other0, other1 = near[1, near_row(j), :], near[1, near_row(j + 1), :]
        state = [factor[mode] * state[mode] + source0 for mode in range(modes)]
        emit(j, state)
        for mode in range(modes):
            both = other0 + factor[mode] * other1
            ahead[pair_rows(shape, half, pair, mode), :] = both
            dot[mode] = dot[mode] + state[mode] * both
        rest = rest + source1 * other1
        ahead[pair_rows(shape, half, pair, modes), :] = other1
        state = [factor[mode] * state[mode] + source1 for mode in range(modes)]
        emit(j + 1, state)
    near_products(shape, *coming, inputs, near)
    return tuple(state), tuple(dot), rest


def second_sweep(shape, half, direction, chunk, square, weight, weight_next, now, state, ahead, conv):
    rows_at = rows_of(shape, half, direction, chunk)
    modes = shape.modes
    state = list(state)
    for j in range(0, shape.chunk, 2):
        pair = shape.length // 2 - 1 - chunk * (shape.chunk // 2) - j // 2
        terms = [weight_next[mode] * state[mode] for mode in range(modes)]
        terms.append(now * ahead[pair_rows(shape, half, pair, modes), :])
        conv[rows_at(j), :] = tree_sum(terms)
        state = [
            square[mode] * state[mode] + ahead[pair_rows(shape, half, pair, mode), :]
            for mode in range(modes)
        ]
        conv[rows_at(j + 1), :] = tree_sum([weight[mode] * state[mode] for mode in range(modes)])
    return tuple(state)


def outputs(shape, half, token, pair, inputs, conv, staged):
    step = min(32, shape.chunk)

    def body(i, carry):
        at = pl.multiple_of(token + i * step, step)
        for group in range(GROUPS):
            lane = slice(group * LANES, (group + 1) * LANES)
            row = half * shape.plane + group * shape.stride + at
            rows = pl.ds(pl.multiple_of(row, GROUPS), step)
            value = conv[rows, :]
            for j in range(2):
                staged[j, half, pl.ds(at, step), lane] = (
                    inputs[2 * pair + j, half, pl.ds(at, step), lane].astype(F32) * value
                ).astype(BF16)
        return carry

    lax.fori_loop(0, shape.chunk // step, body, 0)


def token_of(shape, direction, chunk_index):
    last = shape.chunks - 1
    return pl.multiple_of(
        (chunk_index + direction * (last - 2 * chunk_index)) * shape.chunk, shape.chunk
    )


def in_copy(shape, j, half, direction, chunk, source, inputs, sem):
    rows = pl.ds(token_of(shape, direction, chunk), shape.chunk)
    return pltpu.make_async_copy(
        source.at[rows, lanes_of(half)], inputs.at[j, half, rows, :], sem.at[half * shape.chunks + chunk]
    )


def in_wait(shape, half, direction, chunk, inputs, sem):
    landed = inputs.at[:, half, pl.ds(token_of(shape, direction, chunk), shape.chunk), :]
    pltpu.make_async_copy(landed, landed, sem.at[half * shape.chunks + chunk]).wait()


def out_copy(shape, j, half, direction, chunk, staged, target, sem):
    rows = pl.ds(token_of(shape, direction, chunk), shape.chunk)
    return pltpu.make_async_copy(
        staged.at[j, half, rows, :], target.at[rows, lanes_of(half)], sem
    )


def send_out(shape, half, pair, direction, chunk, staged, targets, sem):
    for p in range(2):

        @pl.when(pair == p)
        def _():
            for j in range(2):
                out_copy(shape, j, half, direction, chunk, staged, targets[2 * p + j], sem).start()


def wait_all(array, sem):
    pltpu.make_async_copy(array, array, sem).wait()


def start_coefficients(rates_hbm, res_hbm, coef, sem):
    pltpu.make_async_copy(rates_hbm, coef.at[0], sem).start()
    pltpu.make_async_copy(res_hbm, coef.at[1], sem).start()


def first_kernel(
    shape, q, dy, v, k, rates_hbm, res_hbm,
    conv, ahead, held, inputs, sent, table, scale,
    near, coef, in_sem, coef_sem,
):
    direction = lax.axis_index("ctx")
    sources = (q, dy, v, k)
    for half in range(shape.halves):
        for chunk in range(shape.chunks):
            for j in range(4):
                in_copy(shape, j, half, direction, chunk, sources[j], inputs, in_sem).start()
            if half + chunk == 0:
                start_coefficients(rates_hbm, res_hbm, coef, coef_sem)
    wait_all(coef, coef_sem)
    scale[...] = mode_tables(coef[0], coef[1], table)
    zeros = (jnp.zeros((GROUPS, LANES), F32),) * shape.modes

    items = shape.halves * shape.chunks

    def run(way):
        in_wait(shape, 0, way, 0, inputs, in_sem)
        near_products(shape, 0, way, 0, 0, inputs, near)

        def sweep(half, _):
            factor = table_rows(table, 0, half, shape.modes, shape.groups)
            weight = table_rows(table, 1, half, shape.modes, shape.groups)

            def body(chunk, carry, weight=weight):
                item = half * shape.chunks + chunk + 1
                coming = jnp.minimum(item, items - 1)
                coming = (coming // shape.chunks, way, coming % shape.chunks)

                @pl.when(item < items)
                def _():
                    in_wait(shape, *coming, inputs, in_sem)

                return first_sweep(
                    shape, half, way, chunk, (*coming, 0), factor, weight, *carry,
                    inputs, near, conv, ahead, held,
                )

            carry = lax.fori_loop(0, shape.chunks - 1, body, (zeros, zeros, zeros[0]))
            state, dot, rest = body(shape.chunks - 1, carry, None)
            for mode in range(shape.modes):
                sent[0, mode, groups_of(half), :] = state[mode].astype(BF16)
                sent[1, mode, groups_of(half), :] = (dot[mode] + rest).astype(BF16)
            return 0

        lax.fori_loop(0, shape.halves, sweep, 0)

    for way in range(2):
        pl.when(direction == way)(functools.partial(run, way))


def early_kernel(shape, conv_in, held, inputs, table, conv, staged):
    del conv_in
    direction = lax.axis_index("ctx")
    step = 16

    def last(half, carry):
        weight = table_rows(table, 1, half, shape.modes, shape.groups)
        rows_at = rows_of(shape, half, direction, shape.chunks - 1)

        def tokens(i, carry):
            for k in range(step):
                j = i * step + k
                conv[rows_at(j), :] = tree_sum(
                    [
                        weight[mode] * held[held_rows(shape, half, j, mode), :]
                        for mode in range(shape.modes)
                    ]
                )
            return carry

        return lax.fori_loop(0, shape.chunk // step, tokens, carry)

    lax.fori_loop(0, shape.halves, last, 0)

    def body(i, carry):
        half, chunk = i // shape.chunks, i % shape.chunks
        outputs(shape, half, token_of(shape, 0, chunk), direction, inputs, conv, staged)
        return carry

    lax.fori_loop(0, shape.halves * shape.chunks, body, 0)


def early_copy(j, half, early, target, sem):
    return pltpu.make_async_copy(
        early.at[j, half], target.at[:, lanes_of(half)], sem
    )


def second_kernel(
    shape, early, ahead, inputs, sent, table, scale, received,
    out0, out1, out2, out3, residue,
    conv, staged, totals, total, out_sem, early_sem, residue_sem,
):
    owner = lax.axis_index("ctx")
    direction = 1 - owner
    targets = (out0, out1, out2, out3)
    modes = shape.modes
    for p in range(2):

        @pl.when(owner == p)
        def _():
            for j in range(2):
                for half in range(shape.halves):
                    early_copy(j, half, early, targets[2 * p + j], early_sem).start()

    def run(way):
        def sweep(half, _):
            factor = table_rows(table, 0, half, modes, shape.groups)
            weight = table_rows(table, 1, half, modes, shape.groups)
            square = [value * value for value in factor]
            weight_next = [weight[mode] * factor[mode] for mode in range(modes)]
            now = tree_sum(weight)
            state = []
            for mode in range(modes):
                mine = sent[0, mode, groups_of(half), :].astype(F32)
                theirs = received[0, mode, groups_of(half), :].astype(F32)
                mine_dot = sent[1, mode, groups_of(half), :].astype(F32)
                their_dot = received[1, mode, groups_of(half), :].astype(F32)
                totals[pl.ds(mode * GROUPS, GROUPS), :] = (
                    mine_dot + their_dot + factor[mode] * (mine * theirs)
                )
                state.append(theirs)
            for group in range(GROUPS):
                lane = lanes_of(half, group)
                total[:, lane] = totals[pl.ds(group, modes, stride=GROUPS), :] * scale[:, lane]
            lane = lanes_of(half)
            pltpu.make_async_copy(total.at[:, lane], residue.at[:, lane], residue_sem).start()

            def body(chunk, state):
                token = token_of(shape, way, chunk)
                state = second_sweep(
                    shape, half, way, chunk, square, weight, weight_next, now, state, ahead, conv
                )
                outputs(shape, half, token, way, inputs, conv, staged)
                for j in range(2):
                    out_copy(
                        shape, j, half, way, chunk, staged, targets[2 * way + j], out_sem
                    ).start()
                return state

            lax.fori_loop(0, shape.chunks, body, tuple(state))
            return 0

        lax.fori_loop(0, shape.halves, sweep, 0)

    for way in range(2):
        pl.when(direction == way)(functools.partial(run, way))

    wait_all(early, early_sem)
    wait_all(total, residue_sem)
    wait_all(staged, out_sem)


def ends_kernel(
    shape, q, dy, v, k, rates_hbm, res_hbm,
    wide, inputs, ends, table, scale,
    coef, in_sem, coef_sem,
):
    sources = (q, dy, v, k)
    start_coefficients(rates_hbm, res_hbm, coef, coef_sem)
    for half in range(shape.halves):
        for chunk in range(shape.chunks):
            for j in range(4):
                in_copy(shape, j, half, 0, chunk, sources[j], inputs, in_sem).start()
    wait_all(coef, coef_sem)
    scale[...] = mode_tables(coef[0], coef[1], table)
    zeros = (jnp.zeros((GROUPS, LANES), F32),) * shape.modes
    for half in range(shape.halves):
        factor = table_rows(table, 0, half, shape.modes, shape.groups)

        def forward(chunk, carry):
            in_wait(shape, half, 0, chunk, inputs, in_sem)
            products(shape, half, token_of(shape, 0, chunk), inputs, wide)
            state, dot = recurrence(
                shape, half, 0, chunk, factor, None, carry[0], carry[1], wide, None
            )
            return tuple(state), tuple(dot)

        def backward(chunk, state):
            state, _ = recurrence(shape, half, 1, chunk, factor, None, state, (), wide, None)
            return tuple(state)

        state, dot = lax.fori_loop(0, shape.chunks, forward, (zeros, zeros))
        back = lax.fori_loop(0, shape.chunks, backward, zeros)
        rows = groups_of(half)
        for mode in range(shape.modes):
            ends[0, mode, rows, :] = state[mode]
            ends[1, mode, rows, :] = back[mode]
            ends[2, mode, rows, :] = dot[mode]


def both_kernel(
    shape, wide, inputs, starts, table,
    out0, out1, out2, out3,
    conv, staged, out_sem,
):
    targets = (out0, out1, out2, out3)
    for direction in range(2):
        for half in range(shape.halves):
            rows = groups_of(half)
            factor = table_rows(table, 0, half, shape.modes, shape.groups)
            weight = table_rows(table, 1, half, shape.modes, shape.groups)
            state = tuple(starts[direction, mode, rows, :] for mode in range(shape.modes))

            def body(chunk, state):
                token = token_of(shape, direction, chunk)
                state, _ = recurrence(
                    shape, half, direction, chunk, factor, weight, state, (), wide, conv
                )
                outputs(shape, half, token, direction, inputs, conv, staged)
                for j in range(2):
                    out_copy(
                        shape, j, half, direction, chunk, staged, targets[2 * direction + j], out_sem
                    ).start()
                return tuple(state)

            lax.fori_loop(0, shape.chunks, body, state)
        wait_all(staged, out_sem)


HBM = pl.BlockSpec(memory_space=pltpu.HBM)
VMEM = pl.BlockSpec(memory_space=pltpu.VMEM)
LIMIT = 24 << 20


def pair(shape, arrays):
    modes, channels = shape.modes, shape.channels
    big = jax.ShapeDtypeStruct((shape.length, channels), BF16)
    copies = shape.halves * shape.chunks
    conv, ahead, held, inputs, sent, table, scale = pl.pallas_call(
        functools.partial(first_kernel, shape),
        in_specs=[HBM] * 6,
        out_specs=[VMEM] * 7,
        out_shape=[
            pltpu.VMEM((shape.rows, LANES), F32),
            pltpu.VMEM((shape.groups * shape.length // 2 * (modes + 1), LANES), F32),
            pltpu.VMEM((shape.groups * shape.chunk * modes, LANES), F32),
            pltpu.VMEM((4, shape.halves, shape.length, BLOCK), BF16),
            jax.ShapeDtypeStruct((2, modes, shape.groups, LANES), BF16),
            pltpu.VMEM((2 * modes * shape.groups, LANES), F32),
            pltpu.VMEM((modes, channels), F32),
        ],
        scratch_shapes=[
            pltpu.VMEM((2, (shape.chunk + PAD) * GROUPS, LANES), F32),
            pltpu.VMEM((2, modes, channels), F32),
            pltpu.SemaphoreType.DMA((copies,)),
            pltpu.SemaphoreType.DMA,
        ],
        compiler_params=pltpu.CompilerParams(vmem_limit_bytes=LIMIT),
        name="first",
    )(*arrays)
    received = lax.ppermute(sent, "ctx", [(0, 1), (1, 0)])
    _, early = pl.pallas_call(
        functools.partial(early_kernel, shape),
        in_specs=[VMEM] * 4,
        out_specs=[VMEM] * 2,
        out_shape=[
            pltpu.VMEM((shape.rows, LANES), F32),
            pltpu.VMEM((2, shape.halves, shape.length, BLOCK), BF16),
        ],
        input_output_aliases={0: 0},
        compiler_params=pltpu.CompilerParams(vmem_limit_bytes=LIMIT),
        name="early",
    )(conv, held, inputs, table)
    *outs, residue = pl.pallas_call(
        functools.partial(second_kernel, shape),
        in_specs=[VMEM] * 7,
        out_specs=[HBM] * 5,
        out_shape=[big] * 4 + [jax.ShapeDtypeStruct((modes, channels), F32)],
        scratch_shapes=[
            pltpu.VMEM((shape.rows, LANES), F32),
            pltpu.VMEM((2, shape.halves, shape.length, BLOCK), BF16),
            pltpu.VMEM((modes * GROUPS, LANES), F32),
            pltpu.VMEM((modes, channels), F32),
            pltpu.SemaphoreType.DMA,
            pltpu.SemaphoreType.DMA,
            pltpu.SemaphoreType.DMA,
        ],
        compiler_params=pltpu.CompilerParams(vmem_limit_bytes=LIMIT),
        name="second",
    )(early, ahead, inputs, sent, table, scale, received)
    return outs, residue


def many(shape, arrays, rates, owners):
    modes, channels = shape.modes, shape.channels
    big = jax.ShapeDtypeStruct((shape.length, channels), BF16)
    copies = shape.halves * shape.chunks
    wide, inputs, ends, table, scale = pl.pallas_call(
        functools.partial(ends_kernel, shape),
        in_specs=[HBM] * 6,
        out_specs=[VMEM] * 5,
        out_shape=[
            pltpu.VMEM((2, shape.rows, LANES), F32),
            pltpu.VMEM((4, shape.halves, shape.length, BLOCK), BF16),
            jax.ShapeDtypeStruct((3, modes, shape.groups, LANES), F32),
            pltpu.VMEM((2 * modes * shape.groups, LANES), F32),
            jax.ShapeDtypeStruct((modes, channels), F32),
        ],
        scratch_shapes=[
            pltpu.VMEM((2, modes, channels), F32),
            pltpu.SemaphoreType.DMA((copies,)),
            pltpu.SemaphoreType.DMA,
        ],
        compiler_params=pltpu.CompilerParams(vmem_limit_bytes=LIMIT),
        name="ends",
    )(*arrays)
    rates = rates.reshape(modes, shape.groups, LANES)
    here = lax.axis_index("ctx")
    parts = lax.all_gather(ends[:2].astype(BF16), "ctx", axis=0).astype(F32)
    owner = jnp.arange(owners, dtype=jnp.int32)
    gaps = jnp.stack([here - 1 - owner, owner - 1 - here], axis=1).astype(F32)[:, :, None, None, None]
    decay = jnp.exp(-rates * shape.length * jnp.maximum(gaps, 0.0))
    starts = jnp.sum(jnp.where(gaps >= 0, decay, 0.0) * parts, axis=0)
    dots = ends[2] + jnp.exp(-rates) * ends[1] * starts[0]
    total = jnp.sum(lax.all_gather(dots.astype(BF16), "ctx", axis=0).astype(F32), axis=0)
    residue = total.reshape(modes, channels) * scale
    outs = pl.pallas_call(
        functools.partial(both_kernel, shape),
        in_specs=[VMEM] * 4,
        out_specs=[HBM] * 4,
        out_shape=[big] * 4,
        scratch_shapes=[
            pltpu.VMEM((shape.rows, LANES), F32),
            pltpu.VMEM((2, shape.halves, shape.length, BLOCK), BF16),
            pltpu.SemaphoreType.DMA,
        ],
        compiler_params=pltpu.CompilerParams(vmem_limit_bytes=LIMIT),
        name="both",
    )(wide, inputs, starts, table)
    return outs, residue


def body(owners, query_branch, key_branch, value_branch, output_grad, residues, decay_rates):
    length, channels = query_branch.shape
    rates = decay_rates.T
    shape = Shape(length, channels, rates.shape[0])
    hbm = functools.partial(pltpu.with_memory_space_constraint, memory_space=pltpu.HBM)
    arrays = [
        hbm(array)
        for array in (query_branch, output_grad, value_branch, key_branch, rates, residues.T)
    ]
    outs, residue = pair(shape, arrays) if owners == 2 else many(shape, arrays, rates, owners)
    mixed_out, query_grad, key_grad, value_grad = outs
    return (mixed_out, query_grad, key_grad, value_grad, residue.T)


def solution(mesh):
    tokens = P(("dp", "ctx"), "tp")
    return jax.shard_map(
        functools.partial(body, mesh.shape["ctx"]),
        mesh=mesh,
        in_specs=(tokens,) * 4 + (P("tp", None),) * 2,
        out_specs=(tokens,) * 4 + (P(("dp", "tp"), None),),
        check_vma=False,
    )
```
